32 devices in a mesh: subj: 4 (over y, x), slab: 8 (over z, core).
Axes of the slice: x: 2, y: 2, z: 4, core: 2. Of those that a mesh axis runs over, the one named last changes fastest.
Arguments:
- source_bricks: bfloat16 [4, 64, 48000], P('subj', 'slab'), may hold values from -6 to 6
- brick_ids: int32 [4, 256], P('subj', 'slab'), may hold values from 0 to 63, as said below
- brick_offsets: int32 [4, 3, 256], P('subj', None, 'slab'), may hold values from 0 to 4
- deformation: float32 [4, 3, 32, 64, 128], P('subj', None, 'slab'), may hold values from -0.3 to 0.3
Outputs:
- atlas_mean: float32 [6, 32, 64, 128], P(None, 'slab', 'subj')
The draws below stay inside these ranges and needn't reach their ends.
Inputs may be any that keep to these rules, and one draw needn't show every extreme that they name: `brick_ids`: brick ids of slab k are k * 8 to (k + 1) * 8 - 1. Among the 32 template pieces of one slab and one subject, at most 6 source bricks lie in any one slab, and in every such list some slab is named exactly 6 times.
All inputs are finite; a program needn't handle non-finite values.
Results may differ from the reference program's by a relative error of at most 0.00095.
Values may be sent and summed in bfloat16 or wider, within the bound.
A program may use at most 128 MiB of HBM per device.

```python
import jax
import jax.numpy as jnp
from jax import lax

COMP = 6
BRICK = 16
PAD = 2
ZQ = 4
BX = 8
BY = 4
NEWTON = 2
NB_ROW = 32
SLAB_Z = 4
SB_DEV = 8
NBT = 64
PIECES = 256
CAP = 6
SUBJECTS = 4
NZ = 32
NY = 64
NX = 128
N_SLAB = 8


def draw_brick_ids(key, part):
    slab_count = PIECES // NB_ROW
    blocks = SUBJECTS * slab_count
    key_heavy, key_rest, key_order, key_local = jax.random.split(key, 4)
    heavy_owner = jax.random.randint(key_heavy, (blocks,), 0, slab_count)
    pool_size = (slab_count - 1) * CAP
    shuffled = jax.vmap(lambda sub_key: jax.random.permutation(sub_key, pool_size))(jax.random.split(key_rest, blocks))
    others = shuffled[:, :NB_ROW - CAP] // CAP
    others = others + (others >= heavy_owner[:, None]).astype(jnp.int32)
    owners = jnp.concatenate([jnp.broadcast_to(heavy_owner[:, None], (blocks, CAP)), others.astype(jnp.int32)], axis=1)
    ordering = jax.vmap(lambda sub_key: jax.random.permutation(sub_key, NB_ROW))(jax.random.split(key_order, blocks))
    owners = jnp.take_along_axis(owners, ordering, axis=1)
    local_index = jax.random.randint(key_local, (blocks, NB_ROW), 0, SB_DEV)
    return (owners * SB_DEV + local_index).reshape(SUBJECTS, PIECES).astype(jnp.int32)


def place_ends(drawn, stream_key, smallest, high):
    index_at = [jax.random.randint(jax.random.fold_in(stream_key, axis), (), 0, length) for axis, length in enumerate(drawn.shape)]
    longest = drawn.shape.index(max(drawn.shape))
    neighbour = index_at[:longest] + [(index_at[longest] + 1) % drawn.shape[longest]] + index_at[longest + 1:]
    return drawn.at[tuple(index_at)].set(smallest).at[tuple(neighbour)].set(high)


def block_scale(rng, dims, cuts, least, largest):
    level, own = 1.0, jax.random.fold_in(rng, 6)
    for position, parts in cuts:
        steps = jnp.exp(jax.random.uniform(jax.random.fold_in(own, position), (parts,), jnp.float32, least / len(cuts), largest / len(cuts)))
        level = level * jnp.repeat(steps, dims[position] // parts).reshape([-1 if axis == position else 1 for axis in range(len(dims))])
    return level


def centred(own_key, extent, spread, most, cuts=(), held_as=jnp.bfloat16):
    array = jax.random.normal(own_key, extent, jnp.float32) * spread
    if len(cuts) > 0:
        array = block_scale(own_key, extent, cuts, -0.22, 0.18) * array
    return jnp.clip(array, min=-most, max=most).astype(held_as)


def setup_inputs(seed: int = 0) -> dict:
    key_list = jax.random.split(jax.random.key(seed), 5)
    return {
        "source_bricks": centred(key_list[0], (SUBJECTS, NBT, COMP * (BRICK + 2 * PAD) ** 3), 1.0, 6.0, ((0, 4), (1, 8))),
        "brick_ids": draw_brick_ids(jax.random.fold_in(key_list[4], 71), 0),
        "brick_offsets": place_ends(jax.random.randint(key_list[2], (SUBJECTS, 3, PIECES), 0, 2 * PAD + 1), jax.random.fold_in(key_list[2], 1), 0, 2 * PAD).astype(jnp.int32),
        "deformation": centred(key_list[3], (SUBJECTS, 3, NZ, NY, NX), 0.1, 0.3, ((0, 4), (2, 8)), jnp.float32),
    }


def crop_window(flat_brick, start_z, start_y, start_x):
    edge_full = BRICK + 2 * PAD
    brick_cube = flat_brick.reshape(COMP, edge_full, edge_full, edge_full)
    anchor = jnp.zeros((), jnp.int32)
    window = lax.dynamic_slice(brick_cube, (anchor, start_z.astype(jnp.int32), start_y.astype(jnp.int32), start_x.astype(jnp.int32)), (COMP, SLAB_Z, BRICK, BRICK))
    return window.reshape(COMP * SLAB_Z * BRICK * BRICK)


def jacobian(rimmed):
    along_z = (rimmed[:, 2:, 1:-1, 1:-1] - rimmed[:, :-2, 1:-1, 1:-1]) * 0.5
    along_y = (rimmed[:, 1:-1, 2:, 1:-1] - rimmed[:, 1:-1, :-2, 1:-1]) * 0.5
    along_x = (rimmed[:, 1:-1, 1:-1, 2:] - rimmed[:, 1:-1, 1:-1, :-2]) * 0.5
    gradients = (along_z, along_y, along_x)
    return [[gradients[col_at][row_at] + (1.0 if row_at == col_at else 0.0) for col_at in range(3)] for row_at in range(3)]


def polar_factor(matrix):
    for newton_step in range(NEWTON):
        cofactor = [[matrix[(row_at + 1) % 3][(col_at + 1) % 3] * matrix[(row_at + 2) % 3][(col_at + 2) % 3]
                     - matrix[(row_at + 1) % 3][(col_at + 2) % 3] * matrix[(row_at + 2) % 3][(col_at + 1) % 3]
                     for col_at in range(3)] for row_at in range(3)]
        determinant = matrix[0][0] * cofactor[0][0] + matrix[0][1] * cofactor[0][1] + matrix[0][2] * cofactor[0][2]
        scaling = 1.0 / determinant
        matrix = [[0.5 * (matrix[row_at][col_at] + cofactor[row_at][col_at] * scaling) for col_at in range(3)] for row_at in range(3)]
    return matrix


def reorient(components, rotation):
    tensor_rows = [[components[0], components[3], components[4]],
                   [components[3], components[1], components[5]],
                   [components[4], components[5], components[2]]]
    left_side = [[rotation[row_at][0] * tensor_rows[0][col_at] + rotation[row_at][1] * tensor_rows[1][col_at]
                  + rotation[row_at][2] * tensor_rows[2][col_at] for col_at in range(3)] for row_at in range(3)]
    pair_list = ((0, 0), (1, 1), (2, 2), (0, 1), (0, 2), (1, 2))
    return [left_side[row_at][0] * rotation[col_at][0] + left_side[row_at][1] * rotation[col_at][1]
            + left_side[row_at][2] * rotation[col_at][2] for row_at, col_at in pair_list]


def reference(source_bricks, brick_ids, brick_offsets, deformation):
    total = jnp.zeros((COMP, NZ, NY, NX), jnp.float32)
    piece_index = jnp.arange(PIECES, dtype=jnp.int32)
    quarter_start = ((piece_index // NB_ROW) % ZQ) * SLAB_Z
    for subject in range(SUBJECTS):
        subject_bricks = source_bricks[subject]
        starts = brick_offsets[subject]

        def cut_piece(brick_id, start_z, start_y, start_x):
            return crop_window(subject_bricks[brick_id], start_z, start_y, start_x)

        windows = jax.vmap(cut_piece)(brick_ids[subject], quarter_start + starts[0], starts[1], starts[2])
        voxel_field = windows.reshape(N_SLAB, BY, BX, COMP, SLAB_Z, BRICK, BRICK)
        voxel_field = voxel_field.transpose(3, 0, 4, 1, 5, 2, 6).reshape(COMP, NZ, NY, NX)
        rimmed = jnp.pad(deformation[subject], ((0, 0), (1, 1), (1, 1), (1, 1)))
        rotation = polar_factor(jacobian(rimmed))
        tensor = voxel_field.astype(jnp.float32)
        rotated = reorient([tensor[channel] for channel in range(COMP)], rotation)
        total = total + jnp.stack(rotated)
    return total / SUBJECTS
```

```python
import jax
import jax.numpy as jnp
from jax import lax
from jax.experimental import pallas as pl
from jax.experimental.pallas import tpu as pltpu
from jax.sharding import PartitionSpec as P

COMP = 6
BRICK = 16
PAD = 2
EDGE = BRICK + 2 * PAD
ZQ = 4
NEWTON = 2
SLAB_Z = 4
LANES = 128
SUB = 8
ROWS = COMP * SLAB_Z
PARTS = ROWS // SUB
BRICK_ROWS = COMP * EDGE
SPAN = 384
FLAT = BRICK * BRICK
ACROSS = LANES // BRICK
BRICK_CHUNKS = 3
U_ROWS = 3 * (SLAB_Z + 2) * BRICK
U_ALL = U_ROWS + 2 * BRICK


def relayout_groups(x_ref, rows_ref, first_group, groups):
    held = x_ref.shape[0]
    lane = lax.broadcasted_iota(jnp.int32, (held, LANES), 1)
    group_lanes = SUB * EDGE * EDGE

    def step(group, carry):
        for m in range(SUB):
            cz = group * SUB + m
            row = cz % EDGE * COMP + cz // EDGE
            shift = 16 * m
            tiles = []
            for j in range(4):
                first = pl.multiple_of(group * group_lanes + (3 * m + j) * LANES, LANES)
                tile = x_ref[:, pl.ds(first, LANES)].astype(jnp.float32)
                tiles.append(pltpu.roll(tile, LANES - shift, 1) if shift else tile)
            for j in range(4):
                value = tiles[j]
                if shift and j < 3:
                    value = jnp.where(lane < LANES - shift, tiles[j], tiles[j + 1])
                rows_ref[j, pl.ds(row, held, stride=BRICK_ROWS), :] = value
        return carry

    lax.fori_loop(first_group, first_group + groups, step, 0)


def selection():
    source = lax.broadcasted_iota(jnp.int32, (SPAN, FLAT), 0)
    target = lax.broadcasted_iota(jnp.int32, (SPAN, FLAT), 1)
    return (source == target // BRICK * EDGE + target % BRICK).astype(jnp.float32).astype(jnp.bfloat16)


def polar_factor(matrix):
    for newton_step in range(NEWTON):
        cofactor = [
            [
                matrix[(a + 1) % 3][(b + 1) % 3] * matrix[(a + 2) % 3][(b + 2) % 3]
                - matrix[(a + 1) % 3][(b + 2) % 3] * matrix[(a + 2) % 3][(b + 1) % 3]
                for b in range(3)
            ]
            for a in range(3)
        ]
        determinant = (
            matrix[0][0] * cofactor[0][0]
            + matrix[0][1] * cofactor[0][1]
            + matrix[0][2] * cofactor[0][2]
        )
        scaling = 0.5 / determinant
        matrix = [
            [0.5 * matrix[a][b] + cofactor[a][b] * scaling for b in range(3)] for a in range(3)
        ]
    return matrix


def reorient(components, rotation):
    tensor_rows = [
        [components[0], components[3], components[4]],
        [components[3], components[1], components[5]],
        [components[4], components[5], components[2]],
    ]
    left_side = [
        [
            rotation[a][0] * tensor_rows[0][b]
            + rotation[a][1] * tensor_rows[1][b]
            + rotation[a][2] * tensor_rows[2][b]
            for b in range(3)
        ]
        for a in range(3)
    ]
    pair_list = ((0, 0), (1, 1), (2, 2), (0, 1), (0, 2), (1, 2))
    return [
        left_side[a][0] * rotation[b][0]
        + left_side[a][1] * rotation[b][1]
        + left_side[a][2] * rotation[b][2]
        for a, b in pair_list
    ]


def rotation_at(load, halo):
    lane = lax.broadcasted_iota(jnp.int32, (BRICK, LANES), 1)
    sub = lax.broadcasted_iota(jnp.int32, (BRICK, LANES), 0)
    matrix = []
    for a in range(3):
        centre = load(a, 1)
        along_z = (load(a, 2) - load(a, 0)) * 0.5
        below = jnp.where(sub == BRICK - 1, halo(a, 1), pltpu.roll(centre, BRICK - 1, 0))
        above = jnp.where(sub == 0, halo(a, 0), pltpu.roll(centre, 1, 0))
        later = jnp.where(lane == LANES - 1, 0.0, pltpu.roll(centre, LANES - 1, 1))
        earlier = jnp.where(lane == 0, 0.0, pltpu.roll(centre, 1, 1))
        gradients = [along_z, (below - above) * 0.5, (later - earlier) * 0.5]
        gradients[a] = gradients[a] + 1.0
        matrix.append(gradients)
    return polar_factor(matrix)


def warp_kernel(
    code_ref, slot_ref, brick_hbm, u_hbm, out_ref,
    asked, bricks, rows_ref, stage, crops, arrived_0, arrived_1, arrived_2,
    u_held, edge_out, edge_in, u_out, u_all, halos, rotations, spread, placed, fields,
    brick_sem, held_sem, own_sem, ask_send, ask_recv, crop_send, crop_recv, edge_send, edge_recv,
    u_send, u_recv, field_send, field_recv,
):
    count, subjects = code_ref.shape[0], fields.shape[0]
    capacity = crops.shape[2]
    half = count // 2
    height = edge_in.shape[1] // 3
    me_s, me_k = lax.axis_index("subj"), lax.axis_index("slab")
    low, high = me_k % half, me_k // half * half
    arrived = (arrived_0, arrived_1, arrived_2)
    barrier = pltpu.get_barrier_semaphore()
    has_before, has_after = me_k > 0, me_k < count - 1

    def reader(side, i):
        return (1 - side) * (half - high) + side * high + (low + i) % half

    def peer_subj(t):
        return (me_s + t) % subjects

    def greet(s, k):
        pl.semaphore_signal(barrier, inc=1, device_id=(s, k), device_id_type=MESH)

    def each_peer(step):
        lax.fori_loop(0, half, lambda i, carry: (step(reader(0, i)), carry)[1], 0)
        lax.fori_loop(1, half, lambda i, carry: (step(reader(1, i)), carry)[1], 0)

    each_peer(lambda k: greet(me_s, k))
    for t in range(1, subjects):
        greet(peer_subj(t), me_k)

    chunk_lanes = brick_hbm.shape[1] // BRICK_CHUNKS

    def load_bricks(c):
        lanes = pl.ds(c * chunk_lanes, chunk_lanes)
        return pltpu.make_async_copy(brick_hbm.at[:, lanes], bricks.at[:, lanes], brick_sem.at[c])

    load_u = pltpu.make_async_copy(u_hbm, u_held, held_sem)
    load_bricks(0).start()
    load_u.start()
    for c in range(1, BRICK_CHUNKS):
        load_bricks(c).start()

    def remote(source, target, send, recv, s, k):
        return pltpu.make_async_remote_copy(
            src_ref=source, dst_ref=target, send_sem=send, recv_sem=recv,
            device_id=(s, k), device_id_type=MESH,
        )

    def ask(k):
        return remote(code_ref.at[k], asked.at[me_k], ask_send.at[k], ask_recv.at[me_k], me_s, k)

    def ask_from(k):
        return remote(code_ref.at[k], asked.at[k], ask_send.at[k], ask_recv.at[k], me_s, k)

    pl.semaphore_wait(barrier, count - 1 + subjects - 1)
    each_peer(lambda k: ask(k).start())
    own_ask = pltpu.make_async_copy(code_ref.at[me_k], asked.at[me_k], own_sem.at[0])
    own_ask.start()

    load_u.wait()
    for a in range(3):
        for side, z in ((0, SLAB_Z - 1), (1, 0)):
            first = (a * SLAB_Z + z) * height
            edge_out[side, a * height:(a + 1) * height] = u_held[first:first + height].astype(jnp.bfloat16)

    edge_down = remote(edge_out.at[0], edge_in.at[0], edge_send.at[0], edge_recv.at[0], me_s, me_k + 1)
    edge_up = remote(edge_out.at[1], edge_in.at[1], edge_send.at[1], edge_recv.at[1], me_s, me_k - 1)

    @pl.when(has_after)
    def _():
        edge_down.start()

    @pl.when(has_before)
    def _():
        edge_up.start()

    groups = BRICK_ROWS // SUB // BRICK_CHUNKS
    for c in range(BRICK_CHUNKS):
        load_bricks(c).wait()
        relayout_groups(bricks, rows_ref, c * groups, groups)
    select = selection()
    lane = lax.broadcasted_iota(jnp.int32, (SUB, LANES), 1)

    each_peer(lambda k: ask_from(k).wait_recv())
    own_ask.wait()

    def give(part, k):
        return remote(
            crops.at[part, k], arrived[part].at[pl.ds(me_k * capacity, capacity)],
            crop_send.at[part, k], crop_recv.at[part, me_k], me_s, k,
        )

    def take(part, k):
        return remote(
            crops.at[part, k], arrived[part].at[pl.ds(k * capacity, capacity)],
            crop_send.at[part, k], crop_recv.at[part, k], me_s, k,
        )

    def cut(code, part):
        start = lax.shift_right_logical(code, 7) + part * SUB
        shift = code & (LANES - 1)
        back = (LANES - shift) & (LANES - 1)
        tiles = [pltpu.roll(rows_ref[j, pl.ds(start, SUB), :], back, 1) for j in range(4)]
        inside = lane < LANES - shift
        return jnp.concatenate([jnp.where(inside, tiles[j], tiles[j + 1]) for j in range(3)], axis=1)

    def crop_side(part, side):

        def collect(i, inner):
            k = reader(side, i)
            for pair in range(capacity // 2):
                both = jnp.concatenate(
                    [cut(asked[k, 0, 2 * pair + n], part) for n in range(2)], axis=0
                )
                row = pl.multiple_of((i * (capacity // 2) + pair) * 2 * SUB, 2 * SUB)
                stage[pl.ds(row, 2 * SUB), :] = both.astype(jnp.bfloat16)
            return inner

        lax.fori_loop(0, half, collect, 0)
        found = jnp.dot(stage[...], select, preferred_element_type=jnp.float32)
        for i in range(half):
            k = reader(side, i)
            for slot in range(capacity):
                first = (i * capacity + slot) * SUB
                piece = found[first:first + SUB]
                tile = jnp.concatenate([piece[:, :LANES], piece[:, LANES:]], axis=0)
                crops[part, k, slot] = tile.astype(jnp.bfloat16)

            if i == 0:
                @pl.when(side == 0)
                def _():
                    give(part, k).start()
            else:
                give(part, k).start()

    for part in range(PARTS):
        lax.fori_loop(0, 2, lambda side, carry, part=part: (crop_side(part, side), carry)[1], 0)

    def keep(part):
        return pltpu.make_async_copy(
            crops.at[part, me_k], arrived[part].at[pl.ds(me_k * capacity, capacity)], own_sem.at[1 + part]
        )

    for part in range(PARTS):
        keep(part).start()

    @pl.when(has_before)
    def _():
        edge_down_in = remote(edge_out.at[0], edge_in.at[0], edge_send.at[0], edge_recv.at[0], me_s, me_k - 1)
        edge_down_in.wait_recv()

    @pl.when(me_k == 0)
    def _():
        edge_in[0] = jnp.zeros(edge_in.shape[1:], jnp.bfloat16)

    @pl.when(has_after)
    def _():
        edge_up_in = remote(edge_out.at[1], edge_in.at[1], edge_send.at[1], edge_recv.at[1], me_s, me_k + 1)
        edge_up_in.wait_recv()

    @pl.when(me_k == count - 1)
    def _():
        edge_in[1] = jnp.zeros(edge_in.shape[1:], jnp.bfloat16)

    def u_block(r):
        return remote(u_out.at[r], u_all.at[me_s], u_send.at[r], u_recv.at[me_s], r, me_k)

    def u_block_from(s):
        return remote(u_out.at[s], u_all.at[s], u_send.at[s], u_recv.at[s], s, me_k)

    blank = jnp.zeros((BRICK - 3 * SLAB_Z, LANES), jnp.float32)
    none = jnp.zeros((3 * SLAB_Z, LANES), jnp.float32)
    for r in range(subjects):
        for a in range(3):
            for z in range(SLAB_Z + 2):
                to = (a * (SLAB_Z + 2) + z) * BRICK
                if z == 0 or z == SLAB_Z + 1:
                    first = a * height + r * BRICK
                    block = edge_in[min(z, 1), first:first + BRICK]
                else:
                    first = (a * SLAB_Z + z - 1) * height + r * BRICK
                    block = u_held[first:first + BRICK].astype(jnp.bfloat16)
                u_out[r, to:to + BRICK] = block
        top, bottom = none, none
        if r > 0:
            top = u_held[pl.ds(r * BRICK - 1, 3 * SLAB_Z, stride=height), :]
        if r < subjects - 1:
            bottom = u_held[pl.ds((r + 1) * BRICK, 3 * SLAB_Z, stride=height), :]
        u_out[r, U_ROWS:U_ALL] = jnp.concatenate([top, blank, bottom, blank], axis=0).astype(jnp.bfloat16)

    for t in range(1, subjects):
        u_block(peer_subj(t)).start()
    own_u = pltpu.make_async_copy(u_out.at[me_s], u_all.at[me_s], own_sem.at[1 + PARTS])
    own_u.start()
    own_u.wait()
    for t in range(1, subjects):
        u_block_from(peer_subj(t)).wait_recv()
    for s in range(subjects):
        halos[s] = u_all[s, U_ROWS:U_ALL].astype(jnp.float32)

    def rotate(at, carry):
        s, z = at // SLAB_Z, at % SLAB_Z

        def load(a, dz):
            first = pl.multiple_of((a * (SLAB_Z + 2) + z + dz) * BRICK, BRICK)
            return u_all[s, pl.ds(first, BRICK), :].astype(jnp.float32)

        def halo(a, side):
            return halos[s, pl.ds(side * BRICK + a * SLAB_Z + z, 1), :]

        rotation = rotation_at(load, halo)
        for a in range(3):
            for b in range(3):
                rotations[s, z, a * 3 + b] = rotation[a][b]
        return carry

    lax.fori_loop(0, subjects * SLAB_Z, rotate, 0)

    group = lax.broadcasted_iota(jnp.int32, (SUB, LANES), 1) // BRICK

    def place(part, r):
        halves = [[], []]
        for j in range(ACROSS):
            tile = arrived[part][slot_ref[r * ACROSS + j]].astype(jnp.float32)
            halves[0].append(tile[:SUB])
            halves[1].append(tile[SUB:])
        for h in range(2):
            pieces = halves[h]
            for bit in (1, 2, 4):
                upper = (group & bit) != 0
                moved = list(pieces)
                for j in range(ACROSS):
                    if j & bit:
                        continue
                    first, second = pieces[j], pieces[j | bit]
                    moved[j] = jnp.where(upper, pltpu.roll(second, BRICK * bit, 1), first)
                    moved[j | bit] = jnp.where(upper, second, pltpu.roll(first, LANES - BRICK * bit, 1))
                pieces = moved
            for y in range(SUB):
                spread[pl.ds(h * SUB + y, SUB, stride=BRICK), :] = pieces[y]
        return spread[...].astype(jnp.bfloat16).reshape(SUB, BRICK, LANES)

    def share(part, r):
        return remote(
            placed.at[part, r], fields.at[me_s, pl.ds(part * SUB, SUB)],
            field_send.at[part, r], field_recv.at[part, me_s], r, me_k,
        )

    def shared_from(part, s):
        return remote(
            placed.at[part, s], fields.at[s, pl.ds(part * SUB, SUB)],
            field_send.at[part, s], field_recv.at[part, s], s, me_k,
        )

    def combine(z):
        total = None
        for s in range(subjects):
            rotation = [[rotations[s, z, a * 3 + b] for b in range(3)] for a in range(3)]
            tensor = [
                fields[s, z * COMP + c].astype(jnp.float32) * (1.0 / subjects) for c in range(COMP)
            ]
            rotated = reorient(tensor, rotation)
            total = rotated if total is None else [total[c] + rotated[c] for c in range(COMP)]
        for c in range(COMP):
            out_ref[c, z] = total[c]

    def finish_part(part):
        for t in range(1, subjects):
            shared_from(part, peer_subj(t)).wait_recv()
        for z in range(SLAB_Z):
            if part * SUB < (z + 1) * COMP <= (part + 1) * SUB:
                combine(z)

    for part in range(PARTS):
        keep(part).wait()
        each_peer(lambda k: take(part, k).wait_recv())

        def place_and_share(t, carry):
            r = peer_subj(t)
            placed[part, r] = place(part, r)
            share(part, r).start()
            return carry

        lax.fori_loop(1, subjects, place_and_share, 0)
        fields[me_s, part * SUB:(part + 1) * SUB] = place(part, me_s)
        if part > 0:
            finish_part(part - 1)

    each_peer(lambda k: ask(k).wait_send())
    for part in range(PARTS):
        each_peer(lambda k: give(part, k).wait_send())
    for t in range(1, subjects):
        u_block(peer_subj(t)).wait_send()

    @pl.when(has_after)
    def _():
        edge_down.wait_send()

    @pl.when(has_before)
    def _():
        edge_up.wait_send()

    finish_part(PARTS - 1)
    for part in range(PARTS):
        for t in range(1, subjects):
            share(part, peer_subj(t)).wait_send()


MESH = pl.DeviceIdType.MESH
VMEM_SPEC = pl.BlockSpec(memory_space=pltpu.VMEM)
SMEM_SPEC = pl.BlockSpec(memory_space=pltpu.SMEM)
HBM_SPEC = pl.BlockSpec(memory_space=pl.ANY)


def slot_tables(brick_ids, brick_offsets, held, slab_count, capacity):
    wanted = brick_ids[0]
    pieces = wanted.shape[0]
    owner, local = wanted // held, wanted % held
    positions = jnp.arange(pieces, dtype=jnp.int32)
    earlier = (owner[:, None] == owner[None, :]) & (positions[None, :] < positions[:, None])
    slot_of = owner * capacity + jnp.sum(earlier.astype(jnp.int32), axis=1)
    start_z = brick_offsets[0, 0] + lax.axis_index("slab") % ZQ * SLAB_Z
    shift = brick_offsets[0, 1] * EDGE + brick_offsets[0, 2]
    code = (local * BRICK_ROWS + start_z * COMP) * LANES + shift
    hits = slot_of[:, None] == jnp.arange(slab_count * capacity, dtype=jnp.int32)[None, :]
    return slot_of, jnp.sum(jnp.where(hits, code[:, None], 0), axis=0)


def shards(source_bricks, brick_ids, brick_offsets, deformation):
    slab_count, subjects = lax.axis_size("slab"), lax.axis_size("subj")
    pieces = brick_ids.shape[1]
    held = source_bricks.shape[1]
    height = deformation.shape[3]
    capacity = max(2, 3 * pieces // (2 * slab_count))
    slot_of, code = slot_tables(brick_ids, brick_offsets, held, slab_count, capacity)
    code = jnp.pad(code.reshape(slab_count, 1, capacity), ((0, 0), (0, 0), (0, LANES - capacity)))
    bf16, f32, dma = jnp.bfloat16, jnp.float32, pltpu.SemaphoreType.DMA
    per_slab, per_part = dma((slab_count,)), dma((PARTS, slab_count))
    return pl.pallas_call(
        warp_kernel,
        out_shape=jax.ShapeDtypeStruct((COMP, SLAB_Z, BRICK, LANES), f32),
        in_specs=[VMEM_SPEC, SMEM_SPEC, HBM_SPEC, HBM_SPEC],
        out_specs=VMEM_SPEC,
        scratch_shapes=[
            pltpu.VMEM((slab_count, 1, LANES), jnp.int32),
            pltpu.VMEM((held, source_bricks.shape[2]), bf16),
            pltpu.VMEM((4, held * BRICK_ROWS, LANES), f32),
            pltpu.VMEM((slab_count // 2 * capacity * SUB, SPAN), bf16),
            pltpu.VMEM((PARTS, slab_count, capacity, BRICK, LANES), bf16),
            *[pltpu.VMEM((slab_count * capacity, BRICK, LANES), bf16)] * PARTS,
            pltpu.VMEM((3 * SLAB_Z * height, LANES), f32),
            pltpu.VMEM((2, 3 * height, LANES), bf16),
            pltpu.VMEM((2, 3 * height, LANES), bf16),
            pltpu.VMEM((subjects, U_ALL, LANES), bf16),
            pltpu.VMEM((subjects, U_ALL, LANES), bf16),
            pltpu.VMEM((subjects, 2 * BRICK, LANES), f32),
            pltpu.VMEM((subjects, SLAB_Z, 9, BRICK, LANES), f32),
            pltpu.VMEM((SUB * BRICK, LANES), f32),
            pltpu.VMEM((PARTS, subjects, SUB, BRICK, LANES), bf16),
            pltpu.VMEM((subjects, ROWS, BRICK, LANES), bf16),
            dma((BRICK_CHUNKS,)), dma, dma((2 + PARTS,)),
            per_slab, per_slab, per_part, per_part, dma((2,)), dma((2,)),
            dma((subjects,)), dma((subjects,)), dma((PARTS, subjects)), dma((PARTS, subjects)),
        ],
        compiler_params=pltpu.CompilerParams(
            vmem_limit_bytes=54784 << 10, collective_id=0, has_side_effects=True
        ),
    )(code, slot_of, source_bricks[0], deformation[0].reshape(-1, LANES))


def solution(mesh):
    in_specs = (
        P("subj", "slab", None),
        P("subj", "slab"),
        P("subj", None, "slab"),
        P("subj", None, "slab", None, None),
    )
    out_specs = P(None, "slab", "subj", None)
    return jax.shard_map(shards, mesh=mesh, in_specs=in_specs, out_specs=out_specs, check_vma=False)
```

```python
import jax
import jax.numpy as jnp
from jax import lax
from jax.experimental import pallas as pl
from jax.experimental.pallas import tpu as pltpu
from jax.sharding import PartitionSpec as P

COMP = 6
BRICK = 16
PAD = 2
EDGE = BRICK + 2 * PAD
ZQ = 4
NEWTON = 2
SLAB_Z = 4
LANES = 128
SUB = 8
ROWS = COMP * SLAB_Z
PARTS = ROWS // SUB
BRICK_ROWS = COMP * EDGE
SPAN = 384
FLAT = BRICK * BRICK
ACROSS = LANES // BRICK
BRICK_CHUNKS = 3
U_ROWS = 3 * (SLAB_Z + 2) * BRICK
U_ALL = U_ROWS + 2 * BRICK
CORES = 2


def relayout_groups(x_ref, rows_ref, first_group, groups):
    held = x_ref.shape[0]
    lane = lax.broadcasted_iota(jnp.int32, (held, LANES), 1)
    group_lanes = SUB * EDGE * EDGE

    def step(group, carry):
        for m in range(SUB):
            cz = group * SUB + m
            row = cz % EDGE * COMP + cz // EDGE
            shift = 16 * m
            tiles = []
            for j in range(4):
                first = pl.multiple_of(group * group_lanes + (3 * m + j) * LANES, LANES)
                tile = x_ref[:, pl.ds(first, LANES)].astype(jnp.float32)
                tiles.append(pltpu.roll(tile, LANES - shift, 1) if shift else tile)
            for j in range(4):
                value = tiles[j]
                if shift and j < 3:
                    value = jnp.where(lane < LANES - shift, tiles[j], tiles[j + 1])
                rows_ref[j, pl.ds(row, held, stride=BRICK_ROWS), :] = value
        return carry

    lax.fori_loop(first_group, first_group + groups, step, 0)


def selection():
    source = lax.broadcasted_iota(jnp.int32, (SPAN, FLAT), 0)
    target = lax.broadcasted_iota(jnp.int32, (SPAN, FLAT), 1)
    return (source == target // BRICK * EDGE + target % BRICK).astype(jnp.float32).astype(jnp.bfloat16)


def polar_factor(matrix):
    for newton_step in range(NEWTON):
        cofactor = [
            [
                matrix[(a + 1) % 3][(b + 1) % 3] * matrix[(a + 2) % 3][(b + 2) % 3]
                - matrix[(a + 1) % 3][(b + 2) % 3] * matrix[(a + 2) % 3][(b + 1) % 3]
                for b in range(3)
            ]
            for a in range(3)
        ]
        determinant = (
            matrix[0][0] * cofactor[0][0]
            + matrix[0][1] * cofactor[0][1]
            + matrix[0][2] * cofactor[0][2]
        )
        scaling = 0.5 / determinant
        matrix = [
            [0.5 * matrix[a][b] + cofactor[a][b] * scaling for b in range(3)] for a in range(3)
        ]
    return matrix


def reorient(components, rotation):
    tensor_rows = [
        [components[0], components[3], components[4]],
        [components[3], components[1], components[5]],
        [components[4], components[5], components[2]],
    ]
    left_side = [
        [
            rotation[a][0] * tensor_rows[0][b]
            + rotation[a][1] * tensor_rows[1][b]
            + rotation[a][2] * tensor_rows[2][b]
            for b in range(3)
        ]
        for a in range(3)
    ]
    pair_list = ((0, 0), (1, 1), (2, 2), (0, 1), (0, 2), (1, 2))
    return [
        left_side[a][0] * rotation[b][0]
        + left_side[a][1] * rotation[b][1]
        + left_side[a][2] * rotation[b][2]
        for a, b in pair_list
    ]


def rotation_at(load, halo):
    lane = lax.broadcasted_iota(jnp.int32, (BRICK, LANES), 1)
    sub = lax.broadcasted_iota(jnp.int32, (BRICK, LANES), 0)
    matrix = []
    for a in range(3):
        centre = load(a, 1)
        along_z = (load(a, 2) - load(a, 0)) * 0.5
        below = jnp.where(sub == BRICK - 1, halo(a, 1), pltpu.roll(centre, BRICK - 1, 0))
        above = jnp.where(sub == 0, halo(a, 0), pltpu.roll(centre, 1, 0))
        later = jnp.where(lane == LANES - 1, 0.0, pltpu.roll(centre, LANES - 1, 1))
        earlier = jnp.where(lane == 0, 0.0, pltpu.roll(centre, 1, 1))
        gradients = [along_z, (below - above) * 0.5, (later - earlier) * 0.5]
        gradients[a] = gradients[a] + 1.0
        matrix.append(gradients)
    return polar_factor(matrix)


def warp_kernel(
    code_ref, slot_ref, brick_hbm, u_hbm, out_ref,
    asked, bricks, rows_ref, stage, crops, arrived_0, arrived_1, arrived_2,
    u_held, edge_out, edge_in, u_out, u_all, halos, rotations, spread, placed, fields,
    seen, opened,
    brick_sem, held_sem, own_sem, ask_send, ask_recv, crop_send, crop_recv, edge_send, edge_recv,
    u_send, u_recv, field_send, field_recv,
):
    count, subjects = code_ref.shape[0], fields.shape[0]
    chips = count // CORES
    capacity = crops.shape[2]
    height = edge_in.shape[1] // 3
    me_s, me_k = lax.axis_index("subj"), lax.axis_index("slab")
    chip, core = me_k // CORES, me_k % CORES
    sibling = me_k + 1 - 2 * core
    arrived = (arrived_0, arrived_1, arrived_2)
    barrier = pltpu.get_barrier_semaphore()
    has_before, has_after = me_k > 0, me_k < count - 1
    bits = [1 << n for n in range(subjects.bit_length() - 1)]

    def peer_subj(t):
        return (me_s + t) % subjects

    def loop(first, last, step):
        lax.fori_loop(first, last, lambda i, carry: (step(i), carry)[1], 0)

    def each_peer(step):
        loop(1, count, lambda t: step((me_k + t) % count))

    def greet(s, k):
        pl.semaphore_signal(barrier, inc=1, device_id=(s, k), device_id_type=MESH)

    greet(me_s, sibling)

    chunk_lanes = brick_hbm.shape[1] // BRICK_CHUNKS

    def load_bricks(c):
        lanes = pl.ds(c * chunk_lanes, chunk_lanes)
        return pltpu.make_async_copy(brick_hbm.at[:, lanes], bricks.at[:, lanes], brick_sem.at[c])

    load_u = pltpu.make_async_copy(u_hbm, u_held, held_sem)
    load_bricks(0).start()
    load_u.start()
    for c in range(1, BRICK_CHUNKS):
        load_bricks(c).start()

    below = (chip + chips - 1) // chips
    lower = sum((me_s // bit) % 2 for bit in bits)
    pl.semaphore_wait(barrier, 1 + below + lower)

    @pl.when(chip < chips - 1)
    def _():
        greet(me_s, me_k + CORES)

    for bit in bits:
        @pl.when((me_s // bit) % 2 == 0)
        def _():
            greet(me_s + bit, me_k)

    loop(0, chip, lambda c: pl.semaphore_signal(
        seen.at[chip], inc=1, device_id=(me_s, (chip - 1 - c) * CORES + core), device_id_type=MESH
    ))

    @pl.when(me_s == subjects - 1)
    def _():
        for s in range(subjects - 1):
            pl.semaphore_signal(opened, inc=1, device_id=(s, me_k), device_id_type=MESH)

    def remote(source, target, send, recv, s, k):
        return pltpu.make_async_remote_copy(
            src_ref=source, dst_ref=target, send_sem=send, recv_sem=recv,
            device_id=(s, k), device_id_type=MESH,
        )

    def ask(k):
        return remote(code_ref.at[k], asked.at[me_k], ask_send.at[k], ask_recv.at[me_k], me_s, k)

    def ask_from(k):
        return remote(code_ref.at[k], asked.at[k], ask_send.at[k], ask_recv.at[k], me_s, k)

    def ask_chip(c):
        for n in range(CORES):
            ask(c * CORES + n).start()

    loop(0, chip, lambda c: ask_chip(chip - 1 - c))
    ask(sibling).start()
    own_ask = pltpu.make_async_copy(code_ref.at[me_k], asked.at[me_k], own_sem.at[0])
    own_ask.start()

    def ask_above(d):
        @pl.when(chip + d < chips)
        def _():
            pl.semaphore_wait(seen.at[chip + d], 1)
            ask_chip(chip + d)

    load_u.wait()
    for a in range(3):
        for side, z in ((0, SLAB_Z - 1), (1, 0)):
            first = (a * SLAB_Z + z) * height
            edge_out[side, a * height:(a + 1) * height] = u_held[first:first + height].astype(jnp.bfloat16)

    edge_down = remote(edge_out.at[0], edge_in.at[0], edge_send.at[0], edge_recv.at[0], me_s, me_k + 1)
    edge_up = remote(edge_out.at[1], edge_in.at[1], edge_send.at[1], edge_recv.at[1], me_s, me_k - 1)

    @pl.when(has_before)
    def _():
        edge_up.start()

    groups = BRICK_ROWS // SUB // BRICK_CHUNKS
    for c in range(BRICK_CHUNKS):
        load_bricks(c).wait()
        relayout_groups(bricks, rows_ref, c * groups, groups)
        if c < BRICK_CHUNKS - 1:
            ask_above(c + 1)
        if c == 0:
            @pl.when(has_after)
            def _():
                edge_down.start()

    loop(BRICK_CHUNKS, chips, ask_above)
    select = selection()
    lane = lax.broadcasted_iota(jnp.int32, (SUB, LANES), 1)
    own_ask.wait()

    def give(part, k):
        return remote(
            crops.at[part, k], arrived[part].at[pl.ds(me_k * capacity, capacity)],
            crop_send.at[part, k], crop_recv.at[part, me_k], me_s, k,
        )

    def take(part, k):
        return remote(
            crops.at[part, k], arrived[part].at[pl.ds(k * capacity, capacity)],
            crop_send.at[part, k], crop_recv.at[part, k], me_s, k,
        )

    def cut(code, part):
        start = lax.shift_right_logical(code, 7) + part * SUB
        shift = code & (LANES - 1)
        back = (LANES - shift) & (LANES - 1)
        tiles = [pltpu.roll(rows_ref[j, pl.ds(start, SUB), :], back, 1) for j in range(4)]
        inside = lane < LANES - shift
        return jnp.concatenate([jnp.where(inside, tiles[j], tiles[j + 1]) for j in range(3)], axis=1)

    side = chips // 2
    upper = chip // side
    near_count = side - 1
    outer = 1 - (chip % (chips - 1) + chips - 2) // (chips - 1)

    def far_at(i):
        return i - outer * near_count

    def unit_chip(i):
        j = far_at(i)
        j = j + outer * (1 - 2 * (j % 2))
        far_chip = (1 - upper) * (side + j) + upper * (side - 1 - j)
        step = i - (1 - outer) * side
        near_chip = upper * side + (chip - upper * side + 1 + step) % side
        is_far = (j >= 0) & (j < side)
        return jnp.where(i == chips - 1, chip, jnp.where(is_far, far_chip, near_chip))

    def serve(i):
        first_reader = unit_chip(i) * CORES
        j = far_at(i)
        inner_far = (outer == 0) & (j >= 0) & (j < side)
        leads = inner_far & (j % 2 == 0)
        follows = inner_far & (j % 2 == 1)
        for n in range(CORES):
            k = first_reader + n

            @pl.when(k != me_k)
            def _():
                ask_from(k).wait_recv()

        for part in range(PARTS):
            for n in range(CORES):
                for pair in range(capacity // 2):
                    both = jnp.concatenate(
                        [cut(asked[first_reader + n, 0, 2 * pair + m], part) for m in range(2)], axis=0
                    )
                    row = ((part * CORES + n) * (capacity // 2) + pair) * 2 * SUB
                    stage[row:row + 2 * SUB, :] = both.astype(jnp.bfloat16)
        found = jnp.dot(stage[...], select, preferred_element_type=jnp.float32)
        for part in range(PARTS):
            for n in range(CORES):
                for slot in range(capacity):
                    first = ((part * CORES + n) * capacity + slot) * SUB
                    piece = found[first:first + SUB]
                    tile = jnp.concatenate([piece[:, :LANES], piece[:, LANES:]], axis=0)
                    crops[part, first_reader + n, slot] = tile.astype(jnp.bfloat16)

        def send(part, first):
            for n in range(CORES):
                @pl.when(first + n != me_k)
                def _():
                    give(part, first + n).start()

        for part in range(1):
            send(part, first_reader)

        @pl.when(jnp.logical_not(leads))
        def _():
            for part in range(1, PARTS):
                send(part, first_reader)

        @pl.when(follows)
        def _():
            for part in range(1, PARTS):
                send(part, unit_chip(i - 1) * CORES)

    serve(0)

    @pl.when(has_before)
    def _():
        edge_down_in = remote(edge_out.at[0], edge_in.at[0], edge_send.at[0], edge_recv.at[0], me_s, me_k - 1)
        edge_down_in.wait_recv()

    @pl.when(me_k == 0)
    def _():
        edge_in[0] = jnp.zeros(edge_in.shape[1:], jnp.bfloat16)

    @pl.when(has_after)
    def _():
        edge_up_in = remote(edge_out.at[1], edge_in.at[1], edge_send.at[1], edge_recv.at[1], me_s, me_k + 1)
        edge_up_in.wait_recv()

    @pl.when(me_k == count - 1)
    def _():
        edge_in[1] = jnp.zeros(edge_in.shape[1:], jnp.bfloat16)

    def u_block(r):
        return remote(u_out.at[r], u_all.at[me_s], u_send.at[r], u_recv.at[me_s], r, me_k)

    def u_block_from(s):
        return remote(u_out.at[s], u_all.at[s], u_send.at[s], u_recv.at[s], s, me_k)

    blank = jnp.zeros((BRICK - 3 * SLAB_Z, LANES), jnp.float32)
    none = jnp.zeros((3 * SLAB_Z, LANES), jnp.float32)
    for r in range(subjects):
        for a in range(3):
            for z in range(SLAB_Z + 2):
                to = (a * (SLAB_Z + 2) + z) * BRICK
                if z == 0 or z == SLAB_Z + 1:
                    first = a * height + r * BRICK
                    block = edge_in[min(z, 1), first:first + BRICK]
                else:
                    first = (a * SLAB_Z + z - 1) * height + r * BRICK
                    block = u_held[first:first + BRICK].astype(jnp.bfloat16)
                u_out[r, to:to + BRICK] = block
        top, bottom = none, none
        if r > 0:
            top = u_held[pl.ds(r * BRICK - 1, 3 * SLAB_Z, stride=height), :]
        if r < subjects - 1:
            bottom = u_held[pl.ds((r + 1) * BRICK, 3 * SLAB_Z, stride=height), :]
        u_out[r, U_ROWS:U_ALL] = jnp.concatenate([top, blank, bottom, blank], axis=0).astype(jnp.bfloat16)

    @pl.when(me_s < subjects - 1)
    def _():
        pl.semaphore_wait(opened, 1)

    for t in range(1, subjects):
        u_block(peer_subj(t)).start()
    own_u = pltpu.make_async_copy(u_out.at[me_s], u_all.at[me_s], own_sem.at[1 + PARTS])
    own_u.start()

    loop(1, chips, serve)

    def keep(part):
        return pltpu.make_async_copy(
            crops.at[part, me_k], arrived[part].at[pl.ds(me_k * capacity, capacity)], own_sem.at[1 + part]
        )

    for part in range(PARTS):
        keep(part).start()

    own_u.wait()
    for t in range(1, subjects):
        u_block_from(peer_subj(t)).wait_recv()
    for s in range(subjects):
        halos[s] = u_all[s, U_ROWS:U_ALL].astype(jnp.float32)

    def rotate(at, carry):
        s, z = at // SLAB_Z, at % SLAB_Z

        def load(a, dz):
            first = pl.multiple_of((a * (SLAB_Z + 2) + z + dz) * BRICK, BRICK)
            return u_all[s, pl.ds(first, BRICK), :].astype(jnp.float32)

        def halo(a, side):
            return halos[s, pl.ds(side * BRICK + a * SLAB_Z + z, 1), :]

        rotation = rotation_at(load, halo)
        for a in range(3):
            for b in range(3):
                rotations[s, z, a * 3 + b] = rotation[a][b]
        return carry

    lax.fori_loop(0, subjects * SLAB_Z, rotate, 0)

    group = lax.broadcasted_iota(jnp.int32, (SUB, LANES), 1) // BRICK

    def place(part, r):
        halves = [[], []]
        for j in range(ACROSS):
            tile = arrived[part][slot_ref[r * ACROSS + j]].astype(jnp.float32)
            halves[0].append(tile[:SUB])
            halves[1].append(tile[SUB:])
        for h in range(2):
            pieces = halves[h]
            for bit in (1, 2, 4):
                upper = (group & bit) != 0
                moved = list(pieces)
                for j in range(ACROSS):
                    if j & bit:
                        continue
                    first, second = pieces[j], pieces[j | bit]
                    moved[j] = jnp.where(upper, pltpu.roll(second, BRICK * bit, 1), first)
                    moved[j | bit] = jnp.where(upper, second, pltpu.roll(first, LANES - BRICK * bit, 1))
                pieces = moved
            for y in range(SUB):
                spread[pl.ds(h * SUB + y, SUB, stride=BRICK), :] = pieces[y]
        return spread[...].astype(jnp.bfloat16).reshape(SUB, BRICK, LANES)

    def share(part, r):
        return remote(
            placed.at[part, r], fields.at[me_s, pl.ds(part * SUB, SUB)],
            field_send.at[part, r], field_recv.at[part, me_s], r, me_k,
        )

    def shared_from(part, s):
        return remote(
            placed.at[part, s], fields.at[s, pl.ds(part * SUB, SUB)],
            field_send.at[part, s], field_recv.at[part, s], s, me_k,
        )

    def combine(z):
        total = None
        for s in range(subjects):
            rotation = [[rotations[s, z, a * 3 + b] for b in range(3)] for a in range(3)]
            tensor = [
                fields[s, z * COMP + c].astype(jnp.float32) * (1.0 / subjects) for c in range(COMP)
            ]
            rotated = reorient(tensor, rotation)
            total = rotated if total is None else [total[c] + rotated[c] for c in range(COMP)]
        for c in range(COMP):
            out_ref[c, z] = total[c]

    def finish_part(part):
        for t in range(1, subjects):
            shared_from(part, peer_subj(t)).wait_recv()
        for z in range(SLAB_Z):
            if part * SUB < (z + 1) * COMP <= (part + 1) * SUB:
                combine(z)

    for part in range(PARTS):
        keep(part).wait()
        each_peer(lambda k: take(part, k).wait_recv())

        def place_and_share(t, carry):
            r = peer_subj(t)
            placed[part, r] = place(part, r)
            share(part, r).start()
            return carry

        lax.fori_loop(1, subjects, place_and_share, 0)
        fields[me_s, part * SUB:(part + 1) * SUB] = place(part, me_s)
        if part > 0:
            finish_part(part - 1)

    each_peer(lambda k: ask(k).wait_send())
    for part in range(PARTS):
        each_peer(lambda k: give(part, k).wait_send())
    for t in range(1, subjects):
        u_block(peer_subj(t)).wait_send()

    @pl.when(has_after)
    def _():
        edge_down.wait_send()

    @pl.when(has_before)
    def _():
        edge_up.wait_send()

    finish_part(PARTS - 1)
    for part in range(PARTS):
        for t in range(1, subjects):
            share(part, peer_subj(t)).wait_send()


MESH = pl.DeviceIdType.MESH
VMEM_SPEC = pl.BlockSpec(memory_space=pltpu.VMEM)
SMEM_SPEC = pl.BlockSpec(memory_space=pltpu.SMEM)
HBM_SPEC = pl.BlockSpec(memory_space=pl.ANY)


def slot_tables(brick_ids, brick_offsets, held, slab_count, capacity):
    wanted = brick_ids[0]
    pieces = wanted.shape[0]
    owner, local = wanted // held, wanted % held
    positions = jnp.arange(pieces, dtype=jnp.int32)
    earlier = (owner[:, None] == owner[None, :]) & (positions[None, :] < positions[:, None])
    slot_of = owner * capacity + jnp.sum(earlier.astype(jnp.int32), axis=1)
    start_z = brick_offsets[0, 0] + lax.axis_index("slab") % ZQ * SLAB_Z
    shift = brick_offsets[0, 1] * EDGE + brick_offsets[0, 2]
    code = (local * BRICK_ROWS + start_z * COMP) * LANES + shift
    hits = slot_of[:, None] == jnp.arange(slab_count * capacity, dtype=jnp.int32)[None, :]
    return slot_of, jnp.sum(jnp.where(hits, code[:, None], 0), axis=0)


def shards(source_bricks, brick_ids, brick_offsets, deformation):
    slab_count, subjects = lax.axis_size("slab"), lax.axis_size("subj")
    pieces = brick_ids.shape[1]
    held = source_bricks.shape[1]
    height = deformation.shape[3]
    capacity = max(2, 3 * pieces // (2 * slab_count))
    slot_of, code = slot_tables(brick_ids, brick_offsets, held, slab_count, capacity)
    code = jnp.pad(code.reshape(slab_count, 1, capacity), ((0, 0), (0, 0), (0, LANES - capacity)))
    bf16, f32, dma = jnp.bfloat16, jnp.float32, pltpu.SemaphoreType.DMA
    regular = pltpu.SemaphoreType.REGULAR
    per_slab, per_part = dma((slab_count,)), dma((PARTS, slab_count))
    return pl.pallas_call(
        warp_kernel,
        out_shape=jax.ShapeDtypeStruct((COMP, SLAB_Z, BRICK, LANES), f32),
        in_specs=[VMEM_SPEC, SMEM_SPEC, HBM_SPEC, HBM_SPEC],
        out_specs=VMEM_SPEC,
        scratch_shapes=[
            pltpu.VMEM((slab_count, 1, LANES), jnp.int32),
            pltpu.VMEM((held, source_bricks.shape[2]), bf16),
            pltpu.VMEM((4, held * BRICK_ROWS, LANES), f32),
            pltpu.VMEM((CORES * capacity * ROWS, SPAN), bf16),
            pltpu.VMEM((PARTS, slab_count, capacity, BRICK, LANES), bf16),
            *[pltpu.VMEM((slab_count * capacity, BRICK, LANES), bf16)] * PARTS,
            pltpu.VMEM((3 * SLAB_Z * height, LANES), f32),
            pltpu.VMEM((2, 3 * height, LANES), bf16),
            pltpu.VMEM((2, 3 * height, LANES), bf16),
            pltpu.VMEM((subjects, U_ALL, LANES), bf16),
            pltpu.VMEM((subjects, U_ALL, LANES), bf16),
            pltpu.VMEM((subjects, 2 * BRICK, LANES), f32),
            pltpu.VMEM((subjects, SLAB_Z, 9, BRICK, LANES), f32),
            pltpu.VMEM((SUB * BRICK, LANES), f32),
            pltpu.VMEM((PARTS, subjects, SUB, BRICK, LANES), bf16),
            pltpu.VMEM((subjects, ROWS, BRICK, LANES), bf16),
            regular((slab_count // CORES,)), regular,
            dma((BRICK_CHUNKS,)), dma, dma((2 + PARTS,)),
            per_slab, per_slab, per_part, per_part, dma((2,)), dma((2,)),
            dma((subjects,)), dma((subjects,)), dma((PARTS, subjects)), dma((PARTS, subjects)),
        ],
        compiler_params=pltpu.CompilerParams(
            vmem_limit_bytes=54784 << 10, collective_id=0, has_side_effects=True
        ),
    )(code, slot_of, source_bricks[0], deformation[0].reshape(-1, LANES))


def solution(mesh):
    in_specs = (
        P("subj", "slab", None),
        P("subj", "slab"),
        P("subj", None, "slab"),
        P("subj", None, "slab", None, None),
    )
    out_specs = P(None, "slab", "subj", None)
    return jax.shard_map(shards, mesh=mesh, in_specs=in_specs, out_specs=out_specs, check_vma=False)
```

```python
import jax
import jax.numpy as jnp
from jax import lax
from jax.experimental import pallas as pl
from jax.experimental.pallas import tpu as pltpu
from jax.sharding import PartitionSpec as P

COMP = 6
BRICK = 16
PAD = 2
EDGE = BRICK + 2 * PAD
ZQ = 4
NEWTON = 2
SLAB_Z = 4
LANES = 128
SUB = 8
ROWS = COMP * SLAB_Z
PARTS = ROWS // SUB
BRICK_ROWS = COMP * EDGE
SPAN = 384
FLAT = BRICK * BRICK
ACROSS = LANES // BRICK
BRICK_CHUNKS = 3
U_ROWS = 3 * (SLAB_Z + 2) * BRICK
U_ALL = U_ROWS + 2 * BRICK
CORES = 2
LEAD = 1


def relayout_groups(x_ref, rows_ref, first_group, groups):
    held = x_ref.shape[0]
    lane = lax.broadcasted_iota(jnp.int32, (held, LANES), 1)
    group_lanes = SUB * EDGE * EDGE

    def step(group, carry):
        for m in range(SUB):
            cz = group * SUB + m
            row = cz % EDGE * COMP + cz // EDGE
            shift = 16 * m
            tiles = []
            for j in range(4):
                first = pl.multiple_of(group * group_lanes + (3 * m + j) * LANES, LANES)
                tile = x_ref[:, pl.ds(first, LANES)].astype(jnp.float32)
                tiles.append(pltpu.roll(tile, LANES - shift, 1) if shift else tile)
            for j in range(4):
                value = tiles[j]
                if shift and j < 3:
                    value = jnp.where(lane < LANES - shift, tiles[j], tiles[j + 1])
                rows_ref[j, pl.ds(row, held, stride=BRICK_ROWS), :] = value
        return carry

    lax.fori_loop(first_group, first_group + groups, step, 0)


def selection():
    source = lax.broadcasted_iota(jnp.int32, (SPAN, FLAT), 0)
    target = lax.broadcasted_iota(jnp.int32, (SPAN, FLAT), 1)
    return (source == target // BRICK * EDGE + target % BRICK).astype(jnp.float32).astype(jnp.bfloat16)


def polar_factor(matrix):
    for newton_step in range(NEWTON):
        cofactor = [
            [
                matrix[(a + 1) % 3][(b + 1) % 3] * matrix[(a + 2) % 3][(b + 2) % 3]
                - matrix[(a + 1) % 3][(b + 2) % 3] * matrix[(a + 2) % 3][(b + 1) % 3]
                for b in range(3)
            ]
            for a in range(3)
        ]
        determinant = (
            matrix[0][0] * cofactor[0][0]
            + matrix[0][1] * cofactor[0][1]
            + matrix[0][2] * cofactor[0][2]
        )
        scaling = 0.5 / determinant
        matrix = [
            [0.5 * matrix[a][b] + cofactor[a][b] * scaling for b in range(3)] for a in range(3)
        ]
    return matrix


def reorient(components, rotation):
    tensor_rows = [
        [components[0], components[3], components[4]],
        [components[3], components[1], components[5]],
        [components[4], components[5], components[2]],
    ]
    left_side = [
        [
            rotation[a][0] * tensor_rows[0][b]
            + rotation[a][1] * tensor_rows[1][b]
            + rotation[a][2] * tensor_rows[2][b]
            for b in range(3)
        ]
        for a in range(3)
    ]
    pair_list = ((0, 0), (1, 1), (2, 2), (0, 1), (0, 2), (1, 2))
    return [
        left_side[a][0] * rotation[b][0]
        + left_side[a][1] * rotation[b][1]
        + left_side[a][2] * rotation[b][2]
        for a, b in pair_list
    ]


def rotation_at(load, halo):
    lane = lax.broadcasted_iota(jnp.int32, (BRICK, LANES), 1)
    sub = lax.broadcasted_iota(jnp.int32, (BRICK, LANES), 0)
    matrix = []
    for a in range(3):
        centre = load(a, 1)
        along_z = (load(a, 2) - load(a, 0)) * 0.5
        below = jnp.where(sub == BRICK - 1, halo(a, 1), pltpu.roll(centre, BRICK - 1, 0))
        above = jnp.where(sub == 0, halo(a, 0), pltpu.roll(centre, 1, 0))
        later = jnp.where(lane == LANES - 1, 0.0, pltpu.roll(centre, LANES - 1, 1))
        earlier = jnp.where(lane == 0, 0.0, pltpu.roll(centre, 1, 1))
        gradients = [along_z, (below - above) * 0.5, (later - earlier) * 0.5]
        gradients[a] = gradients[a] + 1.0
        matrix.append(gradients)
    return polar_factor(matrix)


def slot_tables(ids_ref, offset_ref, held, capacity, me_k):
    pieces = ids_ref.shape[1]
    wanted = ids_ref[...]
    owner, local = wanted // held, wanted % held
    start_z = offset_ref[0] + me_k % ZQ * SLAB_Z
    shift = offset_ref[1] * EDGE + offset_ref[2]
    code = (local * BRICK_ROWS + start_z * COMP) * LANES + shift
    first = lax.broadcasted_iota(jnp.int32, (pieces, pieces), 0)
    second = lax.broadcasted_iota(jnp.int32, (pieces, pieces), 1)

    def upright(row):
        spread = jnp.broadcast_to(row, (pieces, pieces))
        return jnp.sum(jnp.where(first == second, spread, 0), axis=1, keepdims=True)

    owner_up = upright(owner)
    earlier = (owner_up == owner) & (first < second)
    slot = owner * capacity + jnp.sum(earlier.astype(jnp.int32), axis=0, keepdims=True)
    lane = lax.broadcasted_iota(jnp.int32, (pieces, LANES), 1)
    codes = jnp.sum(jnp.where(upright(slot) == lane, upright(code), 0), axis=0, keepdims=True)
    return slot, codes


def warp_kernel(
    ids_hbm, offset_hbm, brick_hbm, u_hbm, out_ref,
    ids_ref, offset_ref, code_ref, slot_row, slot_ref, asked, bricks, rows_ref, stage, crops, arrived_0, arrived_1, arrived_2,
    u_held, edge_out, edge_in, u_out, u_all, halos, rotations, spread, placed, fields,
    seen, opened,
    ids_sem, brick_sem, held_sem, own_sem, ask_send, ask_recv, crop_send, crop_recv, edge_send, edge_recv,
    u_send, u_recv, field_send, field_recv,
):
    count, subjects = asked.shape[0], fields.shape[0]
    chips = count // CORES
    capacity = crops.shape[2]
    height = edge_in.shape[1] // 3
    me_s, me_k = lax.axis_index("subj"), lax.axis_index("slab")
    chip, core = me_k // CORES, me_k % CORES
    sibling = me_k + 1 - 2 * core
    arrived = (arrived_0, arrived_1, arrived_2)
    barrier = pltpu.get_barrier_semaphore()
    has_before, has_after = me_k > 0, me_k < count - 1
    bits = [1 << n for n in range(subjects.bit_length() - 1)]

    def peer_subj(t):
        return (me_s + t) % subjects

    def loop(first, last, step):
        lax.fori_loop(first, last, lambda i, carry: (step(i), carry)[1], 0)

    def each_peer(step):
        loop(1, count, lambda t: step((me_k + t) % count))

    def greet(s, k):
        pl.semaphore_signal(barrier, inc=1, device_id=(s, k), device_id_type=MESH)

    greet(me_s, sibling)
    load_ids = pltpu.make_async_copy(ids_hbm, ids_ref, ids_sem.at[0])
    load_offsets = pltpu.make_async_copy(offset_hbm, offset_ref, ids_sem.at[1])
    load_ids.start()
    load_offsets.start()

    chunk_lanes = brick_hbm.shape[1] // BRICK_CHUNKS

    def load_bricks(c):
        lanes = pl.ds(c * chunk_lanes, chunk_lanes)
        return pltpu.make_async_copy(brick_hbm.at[:, lanes], bricks.at[:, lanes], brick_sem.at[c])

    load_u = pltpu.make_async_copy(u_hbm, u_held, held_sem)
    load_bricks(0).start()
    load_u.start()
    for c in range(1, BRICK_CHUNKS):
        load_bricks(c).start()

    below = (chip + chips - 1) // chips
    lower = sum((me_s // bit) % 2 for bit in bits)
    pl.semaphore_wait(barrier, 1 + below + lower)

    @pl.when(chip < chips - 1)
    def _():
        greet(me_s, me_k + CORES)

    for bit in bits:
        @pl.when((me_s // bit) % 2 == 0)
        def _():
            greet(me_s + bit, me_k)

    loop(0, chip, lambda c: pl.semaphore_signal(
        seen.at[chip], inc=1, device_id=(me_s, (chip - 1 - c) * CORES + core), device_id_type=MESH
    ))

    @pl.when(me_s == subjects - 1)
    def _():
        for s in range(subjects - 1):
            pl.semaphore_signal(opened, inc=1, device_id=(s, me_k), device_id_type=MESH)

    load_ids.wait()
    load_offsets.wait()
    slots, codes = slot_tables(ids_ref, offset_ref, bricks.shape[0], capacity, me_k)
    slot_row[0:1, 0:slots.shape[1]] = slots
    for k in range(count):
        back = (LANES - k * capacity) % LANES
        code_ref[k] = pltpu.roll(codes, back, 1) if back else codes
    load_slots = pltpu.make_async_copy(slot_row, slot_ref, ids_sem.at[2])
    load_slots.start()

    def remote(source, target, send, recv, s, k):
        return pltpu.make_async_remote_copy(
            src_ref=source, dst_ref=target, send_sem=send, recv_sem=recv,
            device_id=(s, k), device_id_type=MESH,
        )

    def ask(k):
        return remote(code_ref.at[k], asked.at[me_k], ask_send.at[k], ask_recv.at[me_k], me_s, k)

    def ask_from(k):
        return remote(code_ref.at[k], asked.at[k], ask_send.at[k], ask_recv.at[k], me_s, k)

    def ask_chip(c):
        for n in range(CORES):
            ask(c * CORES + n).start()

    loop(0, chip, lambda c: ask_chip(chip - 1 - c))
    ask(sibling).start()
    own_ask = pltpu.make_async_copy(code_ref.at[me_k], asked.at[me_k], own_sem.at[0])
    own_ask.start()

    def ask_above(d):
        @pl.when(chip + d < chips)
        def _():
            pl.semaphore_wait(seen.at[chip + d], 1)
            ask_chip(chip + d)

    load_u.wait()
    for a in range(3):
        for side, z in ((0, SLAB_Z - 1), (1, 0)):
            first = (a * SLAB_Z + z) * height
            edge_out[side, a * height:(a + 1) * height] = u_held[first:first + height].astype(jnp.bfloat16)

    edge_down = remote(edge_out.at[0], edge_in.at[0], edge_send.at[0], edge_recv.at[0], me_s, me_k + 1)
    edge_up = remote(edge_out.at[1], edge_in.at[1], edge_send.at[1], edge_recv.at[1], me_s, me_k - 1)

    @pl.when(has_before)
    def _():
        edge_up.start()

    groups = BRICK_ROWS // SUB // BRICK_CHUNKS
    for c in range(BRICK_CHUNKS):
        load_bricks(c).wait()
        relayout_groups(bricks, rows_ref, c * groups, groups)
        if c < BRICK_CHUNKS - 1:
            ask_above(c + 1)
        if c == 0:
            @pl.when(has_after)
            def _():
                edge_down.start()

    loop(BRICK_CHUNKS, chips, ask_above)
    select = selection()
    lane = lax.broadcasted_iota(jnp.int32, (SUB, LANES), 1)
    own_ask.wait()

    def give(part, k):
        return remote(
            crops.at[part, k], arrived[part].at[pl.ds(me_k * capacity, capacity)],
            crop_send.at[part, k], crop_recv.at[part, me_k], me_s, k,
        )

    def take(part, k):
        return remote(
            crops.at[part, k], arrived[part].at[pl.ds(k * capacity, capacity)],
            crop_send.at[part, k], crop_recv.at[part, k], me_s, k,
        )

    def cut(code, part):
        start = lax.shift_right_logical(code, 7) + part * SUB
        shift = code & (LANES - 1)
        back = (LANES - shift) & (LANES - 1)
        tiles = [pltpu.roll(rows_ref[j, pl.ds(start, SUB), :], back, 1) for j in range(4)]
        inside = lane < LANES - shift
        return jnp.concatenate([jnp.where(inside, tiles[j], tiles[j + 1]) for j in range(3)], axis=1)

    side = chips // 2
    upper = chip // side
    near_count = side - 1
    outer = 1 - (chip % (chips - 1) + chips - 2) // (chips - 1)

    def far_at(i):
        return i - outer * near_count

    def unit_chip(i):
        j = far_at(i)
        j = j + outer * (1 - 2 * (j % 2))
        far_chip = (1 - upper) * (side + j) + upper * (side - 1 - j)
        step = i - (1 - outer) * side
        near_chip = upper * side + (chip - upper * side + 1 + step) % side
        is_far = (j >= 0) & (j < side)
        return jnp.where(i == chips - 1, chip, jnp.where(is_far, far_chip, near_chip))

    def serve(i):
        first_reader = unit_chip(i) * CORES
        j = far_at(i)
        inner_far = (outer == 0) & (j >= 0) & (j < side)
        leads = inner_far & (j % 2 == 0)
        follows = inner_far & (j % 2 == 1)
        for n in range(CORES):
            k = first_reader + n

            @pl.when(k != me_k)
            def _():
                ask_from(k).wait_recv()

        codes = [
            [asked[first_reader + n, 0, slot] for slot in range(capacity)] for n in range(CORES)
        ]

        def send(part, first):
            for n in range(CORES):
                @pl.when(first + n != me_k)
                def _():
                    give(part, first + n).start()

        for part in range(PARTS):
            for n in range(CORES):
                for pair in range(capacity // 2):
                    both = jnp.concatenate([cut(codes[n][2 * pair + m], part) for m in range(2)], axis=0)
                    row = (n * (capacity // 2) + pair) * 2 * SUB
                    stage[row:row + 2 * SUB, :] = both.astype(jnp.bfloat16)
            found = jnp.dot(stage[...], select, preferred_element_type=jnp.float32)
            for n in range(CORES):
                for slot in range(capacity):
                    first = (n * capacity + slot) * SUB
                    piece = found[first:first + SUB]
                    tile = jnp.concatenate([piece[:, :LANES], piece[:, LANES:]], axis=0)
                    crops[part, first_reader + n, slot] = tile.astype(jnp.bfloat16)
            if part < LEAD:
                send(part, first_reader)
            else:
                @pl.when(jnp.logical_not(leads))
                def _():
                    send(part, first_reader)

        @pl.when(follows)
        def _():
            for part in range(LEAD, PARTS):
                send(part, unit_chip(i - 1) * CORES)

    serve(0)

    @pl.when(has_before)
    def _():
        edge_down_in = remote(edge_out.at[0], edge_in.at[0], edge_send.at[0], edge_recv.at[0], me_s, me_k - 1)
        edge_down_in.wait_recv()

    @pl.when(me_k == 0)
    def _():
        edge_in[0] = jnp.zeros(edge_in.shape[1:], jnp.bfloat16)

    @pl.when(has_after)
    def _():
        edge_up_in = remote(edge_out.at[1], edge_in.at[1], edge_send.at[1], edge_recv.at[1], me_s, me_k + 1)
        edge_up_in.wait_recv()

    @pl.when(me_k == count - 1)
    def _():
        edge_in[1] = jnp.zeros(edge_in.shape[1:], jnp.bfloat16)

    def u_block(r):
        return remote(u_out.at[r], u_all.at[me_s], u_send.at[r], u_recv.at[me_s], r, me_k)

    def u_block_from(s):
        return remote(u_out.at[s], u_all.at[s], u_send.at[s], u_recv.at[s], s, me_k)

    blank = jnp.zeros((BRICK - 3 * SLAB_Z, LANES), jnp.float32)
    none = jnp.zeros((3 * SLAB_Z, LANES), jnp.float32)
    for r in range(subjects):
        for a in range(3):
            for z in range(SLAB_Z + 2):
                to = (a * (SLAB_Z + 2) + z) * BRICK
                if z == 0 or z == SLAB_Z + 1:
                    first = a * height + r * BRICK
                    block = edge_in[min(z, 1), first:first + BRICK]
                else:
                    first = (a * SLAB_Z + z - 1) * height + r * BRICK
                    block = u_held[first:first + BRICK].astype(jnp.bfloat16)
                u_out[r, to:to + BRICK] = block
        top, bottom = none, none
        if r > 0:
            top = u_held[pl.ds(r * BRICK - 1, 3 * SLAB_Z, stride=height), :]
        if r < subjects - 1:
            bottom = u_held[pl.ds((r + 1) * BRICK, 3 * SLAB_Z, stride=height), :]
        u_out[r, U_ROWS:U_ALL] = jnp.concatenate([top, blank, bottom, blank], axis=0).astype(jnp.bfloat16)

    @pl.when(me_s < subjects - 1)
    def _():
        pl.semaphore_wait(opened, 1)

    for t in range(1, subjects):
        u_block(peer_subj(t)).start()
    own_u = pltpu.make_async_copy(u_out.at[me_s], u_all.at[me_s], own_sem.at[1 + PARTS])
    own_u.start()

    loop(1, chips, serve)

    def keep(part):
        return pltpu.make_async_copy(
            crops.at[part, me_k], arrived[part].at[pl.ds(me_k * capacity, capacity)], own_sem.at[1 + part]
        )

    for part in range(PARTS):
        keep(part).start()

    own_u.wait()
    for t in range(1, subjects):
        u_block_from(peer_subj(t)).wait_recv()
    for s in range(subjects):
        halos[s] = u_all[s, U_ROWS:U_ALL].astype(jnp.float32)

    def rotate(at, carry):
        s, z = at // SLAB_Z, at % SLAB_Z

        def load(a, dz):
            first = pl.multiple_of((a * (SLAB_Z + 2) + z + dz) * BRICK, BRICK)
            return u_all[s, pl.ds(first, BRICK), :].astype(jnp.float32)

        def halo(a, side):
            return halos[s, pl.ds(side * BRICK + a * SLAB_Z + z, 1), :]

        rotation = rotation_at(load, halo)
        for a in range(3):
            for b in range(3):
                rotations[s, z, a * 3 + b] = rotation[a][b]
        return carry

    lax.fori_loop(0, subjects * SLAB_Z, rotate, 0)

    group = lax.broadcasted_iota(jnp.int32, (SUB, LANES), 1) // BRICK

    def place(part, r):
        halves = [[], []]
        for j in range(ACROSS):
            tile = arrived[part][slot_ref[0, r * ACROSS + j]].astype(jnp.float32)
            halves[0].append(tile[:SUB])
            halves[1].append(tile[SUB:])
        for h in range(2):
            pieces = halves[h]
            for bit in (1, 2, 4):
                upper = (group & bit) != 0
                moved = list(pieces)
                for j in range(ACROSS):
                    if j & bit:
                        continue
                    first, second = pieces[j], pieces[j | bit]
                    moved[j] = jnp.where(upper, pltpu.roll(second, BRICK * bit, 1), first)
                    moved[j | bit] = jnp.where(upper, second, pltpu.roll(first, LANES - BRICK * bit, 1))
                pieces = moved
            for y in range(SUB):
                spread[pl.ds(h * SUB + y, SUB, stride=BRICK), :] = pieces[y]
        return spread[...].astype(jnp.bfloat16).reshape(SUB, BRICK, LANES)

    def share(part, r):
        return remote(
            placed.at[part, r], fields.at[me_s, pl.ds(part * SUB, SUB)],
            field_send.at[part, r], field_recv.at[part, me_s], r, me_k,
        )

    def shared_from(part, s):
        return remote(
            placed.at[part, s], fields.at[s, pl.ds(part * SUB, SUB)],
            field_send.at[part, s], field_recv.at[part, s], s, me_k,
        )

    def other(t):
        return t - 1 + (t - 1 + subjects - me_s) // subjects

    def combine(z, s, starts):
        rotation = [[rotations[s, z, a * 3 + b] for b in range(3)] for a in range(3)]
        tensor = [
            fields[s, z * COMP + c].astype(jnp.float32) * (1.0 / subjects) for c in range(COMP)
        ]
        rotated = reorient(tensor, rotation)
        for c in range(COMP):
            out_ref[c, z] = rotated[c] if starts else out_ref[c, z] + rotated[c]

    def combine_part(part, s, starts):
        for z in range(SLAB_Z):
            if part * SUB < (z + 1) * COMP <= (part + 1) * SUB:
                combine(z, s, starts)

    def finish_part(part):
        combine_part(part, me_s, True)
        for t in range(1, subjects):
            shared_from(part, other(t)).wait_recv()
            combine_part(part, other(t), False)

    load_slots.wait()
    for part in range(PARTS):
        keep(part).wait()
        each_peer(lambda k: take(part, k).wait_recv())

        def place_and_share(t, carry):
            r = other(t)
            placed[part, r] = place(part, r)
            share(part, r).start()
            return carry

        lax.fori_loop(1, subjects, place_and_share, 0)
        fields[me_s, part * SUB:(part + 1) * SUB] = place(part, me_s)
        if part > 0:
            finish_part(part - 1)

    each_peer(lambda k: ask(k).wait_send())
    for part in range(PARTS):
        each_peer(lambda k: give(part, k).wait_send())
    for t in range(1, subjects):
        u_block(peer_subj(t)).wait_send()

    @pl.when(has_after)
    def _():
        edge_down.wait_send()

    @pl.when(has_before)
    def _():
        edge_up.wait_send()

    for part in range(PARTS):
        for t in range(1, subjects):
            share(part, other(t)).wait_send()
    finish_part(PARTS - 1)


MESH = pl.DeviceIdType.MESH
VMEM_SPEC = pl.BlockSpec(memory_space=pltpu.VMEM)
HBM_SPEC = pl.BlockSpec(memory_space=pl.ANY)


def shards(source_bricks, brick_ids, brick_offsets, deformation):
    slab_count, subjects = lax.axis_size("slab"), lax.axis_size("subj")
    pieces = brick_ids.shape[1]
    held = source_bricks.shape[1]
    height = deformation.shape[3]
    capacity = max(2, 3 * pieces // (2 * slab_count))
    arguments = [
        brick_ids, brick_offsets.reshape(3, 1, pieces), source_bricks[0],
        deformation[0].reshape(-1, LANES),
    ]
    arguments = [pltpu.with_memory_space_constraint(x, pltpu.HBM) for x in arguments]
    bf16, f32, dma = jnp.bfloat16, jnp.float32, pltpu.SemaphoreType.DMA
    regular = pltpu.SemaphoreType.REGULAR
    per_slab, per_part = dma((slab_count,)), dma((PARTS, slab_count))
    return pl.pallas_call(
        warp_kernel,
        out_shape=jax.ShapeDtypeStruct((COMP, SLAB_Z, BRICK, LANES), f32),
        in_specs=[HBM_SPEC] * 4,
        out_specs=VMEM_SPEC,
        scratch_shapes=[
            pltpu.VMEM((1, pieces), jnp.int32),
            pltpu.VMEM((3, 1, pieces), jnp.int32),
            pltpu.VMEM((slab_count, 1, LANES), jnp.int32),
            pltpu.VMEM((1, LANES), jnp.int32),
            pltpu.SMEM((1, LANES), jnp.int32),
            pltpu.VMEM((slab_count, 1, LANES), jnp.int32),
            pltpu.VMEM((held, source_bricks.shape[2]), bf16),
            pltpu.VMEM((4, held * BRICK_ROWS, LANES), f32),
            pltpu.VMEM((CORES * capacity * SUB, SPAN), bf16),
            pltpu.VMEM((PARTS, slab_count, capacity, BRICK, LANES), bf16),
            *[pltpu.VMEM((slab_count * capacity, BRICK, LANES), bf16)] * PARTS,
            pltpu.VMEM((3 * SLAB_Z * height, LANES), f32),
            pltpu.VMEM((2, 3 * height, LANES), bf16),
            pltpu.VMEM((2, 3 * height, LANES), bf16),
            pltpu.VMEM((subjects, U_ALL, LANES), bf16),
            pltpu.VMEM((subjects, U_ALL, LANES), bf16),
            pltpu.VMEM((subjects, 2 * BRICK, LANES), f32),
            pltpu.VMEM((subjects, SLAB_Z, 9, BRICK, LANES), f32),
            pltpu.VMEM((SUB * BRICK, LANES), f32),
            pltpu.VMEM((PARTS, subjects, SUB, BRICK, LANES), bf16),
            pltpu.VMEM((subjects, ROWS, BRICK, LANES), bf16),
            regular((slab_count // CORES,)), regular,
            dma((3,)), dma((BRICK_CHUNKS,)), dma, dma((2 + PARTS,)),
            per_slab, per_slab, per_part, per_part, dma((2,)), dma((2,)),
            dma((subjects,)), dma((subjects,)), dma((PARTS, subjects)), dma((PARTS, subjects)),
        ],
        compiler_params=pltpu.CompilerParams(
            vmem_limit_bytes=32 << 20, collective_id=0, has_side_effects=True
        ),
    )(*arguments)


def solution(mesh):
    in_specs = (
        P("subj", "slab", None),
        P("subj", "slab"),
        P("subj", None, "slab"),
        P("subj", None, "slab", None, None),
    )
    out_specs = P(None, "slab", "subj", None)
    return jax.shard_map(shards, mesh=mesh, in_specs=in_specs, out_specs=out_specs, check_vma=False)
```

```python
import jax
import jax.numpy as jnp
from jax import lax
from jax.experimental import pallas as pl
from jax.experimental.pallas import tpu as pltpu
from jax.sharding import PartitionSpec as P

COMP = 6
BRICK = 16
PAD = 2
EDGE = BRICK + 2 * PAD
ZQ = 4
NEWTON = 2
SLAB_Z = 4
LANES = 128
SUB = 8
ROWS = COMP * SLAB_Z
PARTS = ROWS // SUB
BRICK_ROWS = COMP * EDGE
SPAN = 384
FLAT = BRICK * BRICK
ACROSS = LANES // BRICK
BRICK_CHUNKS = 3
U_ROWS = 3 * (SLAB_Z + 2) * BRICK
U_ALL = U_ROWS + 2 * BRICK
CORES = 2
LEAD = 1


def relayout_groups(x_ref, rows_ref, first_group, groups):
    held = x_ref.shape[0]
    lane = lax.broadcasted_iota(jnp.int32, (held, LANES), 1)
    group_lanes = SUB * EDGE * EDGE

    def step(group, carry):
        for m in range(SUB):
            cz = group * SUB + m
            row = cz % EDGE * COMP + cz // EDGE
            shift = 16 * m
            tiles = []
            for j in range(4):
                first = pl.multiple_of(group * group_lanes + (3 * m + j) * LANES, LANES)
                tile = x_ref[:, pl.ds(first, LANES)].astype(jnp.float32)
                tiles.append(pltpu.roll(tile, LANES - shift, 1) if shift else tile)
            for j in range(4):
                value = tiles[j]
                if shift and j < 3:
                    value = jnp.where(lane < LANES - shift, tiles[j], tiles[j + 1])
                rows_ref[j, pl.ds(row, held, stride=BRICK_ROWS), :] = value
        return carry

    lax.fori_loop(first_group, first_group + groups, step, 0)


def selection():
    source = lax.broadcasted_iota(jnp.int32, (SPAN, FLAT), 0)
    target = lax.broadcasted_iota(jnp.int32, (SPAN, FLAT), 1)
    return (source == target // BRICK * EDGE + target % BRICK).astype(jnp.float32).astype(jnp.bfloat16)


def polar_factor(matrix):
    for newton_step in range(NEWTON):
        cofactor = [
            [
                matrix[(a + 1) % 3][(b + 1) % 3] * matrix[(a + 2) % 3][(b + 2) % 3]
                - matrix[(a + 1) % 3][(b + 2) % 3] * matrix[(a + 2) % 3][(b + 1) % 3]
                for b in range(3)
            ]
            for a in range(3)
        ]
        determinant = (
            matrix[0][0] * cofactor[0][0]
            + matrix[0][1] * cofactor[0][1]
            + matrix[0][2] * cofactor[0][2]
        )
        scaling = 0.5 / determinant
        matrix = [
            [0.5 * matrix[a][b] + cofactor[a][b] * scaling for b in range(3)] for a in range(3)
        ]
    return matrix


def reorient(components, rotation):
    tensor_rows = [
        [components[0], components[3], components[4]],
        [components[3], components[1], components[5]],
        [components[4], components[5], components[2]],
    ]
    left_side = [
        [
            rotation[a][0] * tensor_rows[0][b]
            + rotation[a][1] * tensor_rows[1][b]
            + rotation[a][2] * tensor_rows[2][b]
            for b in range(3)
        ]
        for a in range(3)
    ]
    pair_list = ((0, 0), (1, 1), (2, 2), (0, 1), (0, 2), (1, 2))
    return [
        left_side[a][0] * rotation[b][0]
        + left_side[a][1] * rotation[b][1]
        + left_side[a][2] * rotation[b][2]
        for a, b in pair_list
    ]


def rotation_at(load, halo):
    lane = lax.broadcasted_iota(jnp.int32, (BRICK, LANES), 1)
    sub = lax.broadcasted_iota(jnp.int32, (BRICK, LANES), 0)
    matrix = []
    for a in range(3):
        centre = load(a, 1)
        along_z = (load(a, 2) - load(a, 0)) * 0.5
        below = jnp.where(sub == BRICK - 1, halo(a, 1), pltpu.roll(centre, BRICK - 1, 0))
        above = jnp.where(sub == 0, halo(a, 0), pltpu.roll(centre, 1, 0))
        later = jnp.where(lane == LANES - 1, 0.0, pltpu.roll(centre, LANES - 1, 1))
        earlier = jnp.where(lane == 0, 0.0, pltpu.roll(centre, 1, 1))
        gradients = [along_z, (below - above) * 0.5, (later - earlier) * 0.5]
        gradients[a] = gradients[a] + 1.0
        matrix.append(gradients)
    return polar_factor(matrix)


def slot_tables(ids_ref, offset_ref, held, capacity, me_k):
    pieces = ids_ref.shape[1]
    wanted = ids_ref[...]
    owner, local = wanted // held, wanted % held
    start_z = offset_ref[0] + me_k % ZQ * SLAB_Z
    shift = offset_ref[1] * EDGE + offset_ref[2]
    code = (local * BRICK_ROWS + start_z * COMP) * LANES + shift
    first = lax.broadcasted_iota(jnp.int32, (pieces, pieces), 0)
    second = lax.broadcasted_iota(jnp.int32, (pieces, pieces), 1)

    def upright(row):
        spread = jnp.broadcast_to(row, (pieces, pieces))
        return jnp.sum(jnp.where(first == second, spread, 0), axis=1, keepdims=True)

    owner_up = upright(owner)
    earlier = (owner_up == owner) & (first < second)
    slot = owner * capacity + jnp.sum(earlier.astype(jnp.int32), axis=0, keepdims=True)
    lane = lax.broadcasted_iota(jnp.int32, (pieces, LANES), 1)
    codes = jnp.sum(jnp.where(upright(slot) == lane, upright(code), 0), axis=0, keepdims=True)
    return slot, codes


def warp_kernel(
    ids_hbm, offset_hbm, brick_hbm, u_hbm, out_ref,
    ids_ref, offset_ref, code_ref, slot_row, slot_ref, asked, bricks, rows_ref, stage, crops, arrived_0, arrived_1, arrived_2,
    u_held, edge_out, edge_in, u_out, u_all, halos, rotations, spread, placed, fields,
    seen, opened,
    ids_sem, brick_sem, held_sem, own_sem, ask_send, ask_recv, crop_send, crop_recv, edge_send, edge_recv,
    u_send, u_recv, field_send, field_recv,
):
    count, subjects = asked.shape[0], fields.shape[0]
    chips = count // CORES
    capacity = crops.shape[2]
    height = edge_in.shape[1] // 3
    me_s, me_k = lax.axis_index("subj"), lax.axis_index("slab")
    chip, core = me_k // CORES, me_k % CORES
    sibling = me_k + 1 - 2 * core
    arrived = (arrived_0, arrived_1, arrived_2)
    barrier = pltpu.get_barrier_semaphore()
    has_before, has_after = me_k > 0, me_k < count - 1
    bits = [1 << n for n in range(subjects.bit_length() - 1)]

    def peer_subj(t):
        return (me_s + t) % subjects

    def loop(first, last, step):
        lax.fori_loop(first, last, lambda i, carry: (step(i), carry)[1], 0)

    def each_peer(step):
        loop(1, count, lambda t: step((me_k + t) % count))

    def greet(s, k):
        pl.semaphore_signal(barrier, inc=1, device_id=(s, k), device_id_type=MESH)

    greet(me_s, sibling)
    load_ids = pltpu.make_async_copy(ids_hbm, ids_ref, ids_sem.at[0])
    load_offsets = pltpu.make_async_copy(offset_hbm, offset_ref, ids_sem.at[1])
    load_ids.start()
    load_offsets.start()

    chunk_lanes = brick_hbm.shape[1] // BRICK_CHUNKS

    def load_bricks(c):
        lanes = pl.ds(c * chunk_lanes, chunk_lanes)
        return pltpu.make_async_copy(brick_hbm.at[:, lanes], bricks.at[:, lanes], brick_sem.at[c])

    load_u = pltpu.make_async_copy(u_hbm, u_held, held_sem)
    load_bricks(0).start()
    load_u.start()
    for c in range(1, BRICK_CHUNKS):
        load_bricks(c).start()

    below = (chip + chips - 1) // chips
    lower = sum((me_s // bit) % 2 for bit in bits)
    pl.semaphore_wait(barrier, 1 + below + lower)

    @pl.when(chip < chips - 1)
    def _():
        greet(me_s, me_k + CORES)

    for bit in bits:
        @pl.when((me_s // bit) % 2 == 0)
        def _():
            greet(me_s + bit, me_k)

    loop(0, chip, lambda c: pl.semaphore_signal(
        seen.at[chip], inc=1, device_id=(me_s, (chip - 1 - c) * CORES + core), device_id_type=MESH
    ))

    @pl.when(me_s == subjects - 1)
    def _():
        for s in range(subjects - 1):
            pl.semaphore_signal(opened, inc=1, device_id=(s, me_k), device_id_type=MESH)

    load_ids.wait()
    load_offsets.wait()
    slots, codes = slot_tables(ids_ref, offset_ref, bricks.shape[0], capacity, me_k)
    slot_row[0:1, 0:slots.shape[1]] = slots
    for k in range(count):
        back = (LANES - k * capacity) % LANES
        code_ref[k] = pltpu.roll(codes, back, 1) if back else codes
    load_slots = pltpu.make_async_copy(slot_row, slot_ref, ids_sem.at[2])
    load_slots.start()

    def remote(source, target, send, recv, s, k):
        return pltpu.make_async_remote_copy(
            src_ref=source, dst_ref=target, send_sem=send, recv_sem=recv,
            device_id=(s, k), device_id_type=MESH,
        )

    def ask(k):
        return remote(code_ref.at[k], asked.at[me_k], ask_send.at[k], ask_recv.at[me_k], me_s, k)

    def ask_from(k):
        return remote(code_ref.at[k], asked.at[k], ask_send.at[k], ask_recv.at[k], me_s, k)

    def ask_chip(c):
        for n in range(CORES):
            ask(c * CORES + n).start()

    loop(0, chip, lambda c: ask_chip(chip - 1 - c))
    ask(sibling).start()
    own_ask = pltpu.make_async_copy(code_ref.at[me_k], asked.at[me_k], own_sem.at[0])
    own_ask.start()

    def ask_above(d):
        @pl.when(chip + d < chips)
        def _():
            pl.semaphore_wait(seen.at[chip + d], 1)
            ask_chip(chip + d)

    load_u.wait()
    for a in range(3):
        for side, z in ((0, SLAB_Z - 1), (1, 0)):
            first = (a * SLAB_Z + z) * height
            edge_out[side, a * height:(a + 1) * height] = u_held[first:first + height].astype(jnp.bfloat16)

    edge_down = remote(edge_out.at[0], edge_in.at[0], edge_send.at[0], edge_recv.at[0], me_s, me_k + 1)
    edge_up = remote(edge_out.at[1], edge_in.at[1], edge_send.at[1], edge_recv.at[1], me_s, me_k - 1)

    @pl.when(has_before)
    def _():
        edge_up.start()

    groups = BRICK_ROWS // SUB // BRICK_CHUNKS
    for c in range(BRICK_CHUNKS):
        load_bricks(c).wait()
        relayout_groups(bricks, rows_ref, c * groups, groups)
        if c < BRICK_CHUNKS - 1:
            ask_above(c + 1)
        if c == 0:
            @pl.when(has_after)
            def _():
                edge_down.start()

    loop(BRICK_CHUNKS, chips, ask_above)
    select = selection()
    lane = lax.broadcasted_iota(jnp.int32, (SUB, LANES), 1)
    own_ask.wait()

    def give(part, k):
        return remote(
            crops.at[part, k], arrived[part].at[pl.ds(me_k * capacity, capacity)],
            crop_send.at[part, k], crop_recv.at[part, me_k], me_s, k,
        )

    def take(part, k):
        return remote(
            crops.at[part, k], arrived[part].at[pl.ds(k * capacity, capacity)],
            crop_send.at[part, k], crop_recv.at[part, k], me_s, k,
        )

    def cut(code, part):
        start = lax.shift_right_logical(code, 7) + part * SUB
        shift = code & (LANES - 1)
        back = (LANES - shift) & (LANES - 1)
        tiles = [pltpu.roll(rows_ref[j, pl.ds(start, SUB), :], back, 1) for j in range(4)]
        inside = lane < LANES - shift
        return jnp.concatenate([jnp.where(inside, tiles[j], tiles[j + 1]) for j in range(3)], axis=1)

    side = chips // 2
    upper = chip // side
    near_count = side - 1
    outer = 1 - (chip % (chips - 1) + chips - 2) // (chips - 1)

    early = 1 - (1 - outer) * upper

    def far_at(i):
        return i - early * near_count

    def unit_chip(i):
        j = far_at(i)
        j = j + outer * (1 - 2 * (j % 2))
        far_chip = (1 - upper) * (side + j) + upper * (side - 1 - j)
        step = i - (1 - early) * side
        near_chip = upper * side + (chip - upper * side + 1 + step) % side
        is_far = (j >= 0) & (j < side)
        return jnp.where(i == chips - 1, chip, jnp.where(is_far, far_chip, near_chip))

    def serve(i):
        first_reader = unit_chip(i) * CORES
        j = far_at(i)
        inner_far = (outer == 0) & (j >= 0) & (j < side)
        leads = inner_far & (j % 2 == 0)
        follows = inner_far & (j % 2 == 1)
        for n in range(CORES):
            k = first_reader + n

            @pl.when(k != me_k)
            def _():
                ask_from(k).wait_recv()

        codes = [
            [asked[first_reader + n, 0, slot] for slot in range(capacity)] for n in range(CORES)
        ]

        def send(part, first):
            for n in range(CORES):
                @pl.when(first + n != me_k)
                def _():
                    give(part, first + n).start()

        for part in range(PARTS):
            for n in range(CORES):
                for pair in range(capacity // 2):
                    both = jnp.concatenate([cut(codes[n][2 * pair + m], part) for m in range(2)], axis=0)
                    row = (n * (capacity // 2) + pair) * 2 * SUB
                    stage[row:row + 2 * SUB, :] = both.astype(jnp.bfloat16)
            found = jnp.dot(stage[...], select, preferred_element_type=jnp.float32)
            for n in range(CORES):
                for slot in range(capacity):
                    first = (n * capacity + slot) * SUB
                    piece = found[first:first + SUB]
                    tile = jnp.concatenate([piece[:, :LANES], piece[:, LANES:]], axis=0)
                    crops[part, first_reader + n, slot] = tile.astype(jnp.bfloat16)
            if part < LEAD:
                send(part, first_reader)
            else:
                @pl.when(jnp.logical_not(leads))
                def _():
                    send(part, first_reader)

        @pl.when(follows)
        def _():
            for part in range(LEAD, PARTS):
                send(part, unit_chip(i - 1) * CORES)

    def u_block(r):
        return remote(u_out.at[r], u_all.at[me_s], u_send.at[r], u_recv.at[me_s], r, me_k)

    def u_block_from(s):
        return remote(u_out.at[s], u_all.at[s], u_send.at[s], u_recv.at[s], s, me_k)

    own_u = pltpu.make_async_copy(u_out.at[me_s], u_all.at[me_s], own_sem.at[1 + PARTS])

    def hand_u():
        @pl.when(has_before)
        def _():
            edge_down_in = remote(edge_out.at[0], edge_in.at[0], edge_send.at[0], edge_recv.at[0], me_s, me_k - 1)
            edge_down_in.wait_recv()

        @pl.when(me_k == 0)
        def _():
            edge_in[0] = jnp.zeros(edge_in.shape[1:], jnp.bfloat16)

        @pl.when(has_after)
        def _():
            edge_up_in = remote(edge_out.at[1], edge_in.at[1], edge_send.at[1], edge_recv.at[1], me_s, me_k + 1)
            edge_up_in.wait_recv()

        @pl.when(me_k == count - 1)
        def _():
            edge_in[1] = jnp.zeros(edge_in.shape[1:], jnp.bfloat16)

        blank = jnp.zeros((BRICK - 3 * SLAB_Z, LANES), jnp.float32)
        none = jnp.zeros((3 * SLAB_Z, LANES), jnp.float32)
        for r in range(subjects):
            for a in range(3):
                for z in range(SLAB_Z + 2):
                    to = (a * (SLAB_Z + 2) + z) * BRICK
                    if z == 0 or z == SLAB_Z + 1:
                        first = a * height + r * BRICK
                        block = edge_in[min(z, 1), first:first + BRICK]
                    else:
                        first = (a * SLAB_Z + z - 1) * height + r * BRICK
                        block = u_held[first:first + BRICK].astype(jnp.bfloat16)
                    u_out[r, to:to + BRICK] = block
            top, bottom = none, none
            if r > 0:
                top = u_held[pl.ds(r * BRICK - 1, 3 * SLAB_Z, stride=height), :]
            if r < subjects - 1:
                bottom = u_held[pl.ds((r + 1) * BRICK, 3 * SLAB_Z, stride=height), :]
            u_out[r, U_ROWS:U_ALL] = jnp.concatenate([top, blank, bottom, blank], axis=0).astype(jnp.bfloat16)

        @pl.when(me_s < subjects - 1)
        def _():
            pl.semaphore_wait(opened, 1)

        for t in range(1, subjects):
            u_block(peer_subj(t)).start()
        own_u.start()

    def serve_and_hand(i):
        serve(i)

        @pl.when(i == (1 - outer) * (1 + early))
        def _():
            hand_u()

    loop(0, chips, serve_and_hand)

    def keep(part):
        return pltpu.make_async_copy(
            crops.at[part, me_k], arrived[part].at[pl.ds(me_k * capacity, capacity)], own_sem.at[1 + part]
        )

    for part in range(PARTS):
        keep(part).start()

    own_u.wait()
    for t in range(1, subjects):
        u_block_from(peer_subj(t)).wait_recv()
    for s in range(subjects):
        halos[s] = u_all[s, U_ROWS:U_ALL].astype(jnp.float32)

    def rotate(at, carry):
        s, z = at // SLAB_Z, at % SLAB_Z

        def load(a, dz):
            first = pl.multiple_of((a * (SLAB_Z + 2) + z + dz) * BRICK, BRICK)
            return u_all[s, pl.ds(first, BRICK), :].astype(jnp.float32)

        def halo(a, side):
            return halos[s, pl.ds(side * BRICK + a * SLAB_Z + z, 1), :]

        rotation = rotation_at(load, halo)
        for a in range(3):
            for b in range(3):
                rotations[s, z, a * 3 + b] = rotation[a][b]
        return carry

    lax.fori_loop(0, subjects * SLAB_Z, rotate, 0)

    group = lax.broadcasted_iota(jnp.int32, (SUB, LANES), 1) // BRICK

    def place(part, r):
        halves = [[], []]
        for j in range(ACROSS):
            tile = arrived[part][slot_ref[0, r * ACROSS + j]].astype(jnp.float32)
            halves[0].append(tile[:SUB])
            halves[1].append(tile[SUB:])
        for h in range(2):
            pieces = halves[h]
            for bit in (1, 2, 4):
                upper = (group & bit) != 0
                moved = list(pieces)
                for j in range(ACROSS):
                    if j & bit:
                        continue
                    first, second = pieces[j], pieces[j | bit]
                    moved[j] = jnp.where(upper, pltpu.roll(second, BRICK * bit, 1), first)
                    moved[j | bit] = jnp.where(upper, second, pltpu.roll(first, LANES - BRICK * bit, 1))
                pieces = moved
            for y in range(SUB):
                spread[pl.ds(h * SUB + y, SUB, stride=BRICK), :] = pieces[y]
        return spread[...].astype(jnp.bfloat16).reshape(SUB, BRICK, LANES)

    def share(part, r):
        return remote(
            placed.at[part, r], fields.at[me_s, pl.ds(part * SUB, SUB)],
            field_send.at[part, r], field_recv.at[part, me_s], r, me_k,
        )

    def shared_from(part, s):
        return remote(
            placed.at[part, s], fields.at[s, pl.ds(part * SUB, SUB)],
            field_send.at[part, s], field_recv.at[part, s], s, me_k,
        )

    def other(t):
        return t - 1 + (t - 1 + subjects - me_s) // subjects

    def combine(z, s, starts):
        rotation = [[rotations[s, z, a * 3 + b] for b in range(3)] for a in range(3)]
        tensor = [
            fields[s, z * COMP + c].astype(jnp.float32) * (1.0 / subjects) for c in range(COMP)
        ]
        rotated = reorient(tensor, rotation)
        for c in range(COMP):
            out_ref[c, z] = rotated[c] if starts else out_ref[c, z] + rotated[c]

    def combine_part(part, s, starts):
        for z in range(SLAB_Z):
            if part * SUB < (z + 1) * COMP <= (part + 1) * SUB:
                combine(z, s, starts)

    def finish_part(part):
        combine_part(part, me_s, True)
        for t in range(1, subjects):
            shared_from(part, other(t)).wait_recv()
            combine_part(part, other(t), False)

    load_slots.wait()
    for part in range(PARTS):
        keep(part).wait()
        each_peer(lambda k: take(part, k).wait_recv())

        def place_and_share(t, carry):
            r = other(t)
            placed[part, r] = place(part, r)
            share(part, r).start()
            return carry

        lax.fori_loop(1, subjects, place_and_share, 0)
        fields[me_s, part * SUB:(part + 1) * SUB] = place(part, me_s)
        if part > 0:
            finish_part(part - 1)

    each_peer(lambda k: ask(k).wait_send())
    for part in range(PARTS):
        each_peer(lambda k: give(part, k).wait_send())
    for t in range(1, subjects):
        u_block(peer_subj(t)).wait_send()

    @pl.when(has_after)
    def _():
        edge_down.wait_send()

    @pl.when(has_before)
    def _():
        edge_up.wait_send()

    for part in range(PARTS):
        for t in range(1, subjects):
            share(part, other(t)).wait_send()
    finish_part(PARTS - 1)


MESH = pl.DeviceIdType.MESH
VMEM_SPEC = pl.BlockSpec(memory_space=pltpu.VMEM)
HBM_SPEC = pl.BlockSpec(memory_space=pl.ANY)


def shards(source_bricks, brick_ids, brick_offsets, deformation):
    slab_count, subjects = lax.axis_size("slab"), lax.axis_size("subj")
    pieces = brick_ids.shape[1]
    held = source_bricks.shape[1]
    height = deformation.shape[3]
    capacity = max(2, 3 * pieces // (2 * slab_count))
    arguments = [
        brick_ids, brick_offsets.reshape(3, 1, pieces), source_bricks[0],
        deformation[0].reshape(-1, LANES),
    ]
    arguments = [pltpu.with_memory_space_constraint(x, pltpu.HBM) for x in arguments]
    bf16, f32, dma = jnp.bfloat16, jnp.float32, pltpu.SemaphoreType.DMA
    regular = pltpu.SemaphoreType.REGULAR
    per_slab, per_part = dma((slab_count,)), dma((PARTS, slab_count))
    return pl.pallas_call(
        warp_kernel,
        out_shape=jax.ShapeDtypeStruct((COMP, SLAB_Z, BRICK, LANES), f32),
        in_specs=[HBM_SPEC] * 4,
        out_specs=VMEM_SPEC,
        scratch_shapes=[
            pltpu.VMEM((1, pieces), jnp.int32),
            pltpu.VMEM((3, 1, pieces), jnp.int32),
            pltpu.VMEM((slab_count, 1, LANES), jnp.int32),
            pltpu.VMEM((1, LANES), jnp.int32),
            pltpu.SMEM((1, LANES), jnp.int32),
            pltpu.VMEM((slab_count, 1, LANES), jnp.int32),
            pltpu.VMEM((held, source_bricks.shape[2]), bf16),
            pltpu.VMEM((4, held * BRICK_ROWS, LANES), f32),
            pltpu.VMEM((CORES * capacity * SUB, SPAN), bf16),
            pltpu.VMEM((PARTS, slab_count, capacity, BRICK, LANES), bf16),
            *[pltpu.VMEM((slab_count * capacity, BRICK, LANES), bf16)] * PARTS,
            pltpu.VMEM((3 * SLAB_Z * height, LANES), f32),
            pltpu.VMEM((2, 3 * height, LANES), bf16),
            pltpu.VMEM((2, 3 * height, LANES), bf16),
            pltpu.VMEM((subjects, U_ALL, LANES), bf16),
            pltpu.VMEM((subjects, U_ALL, LANES), bf16),
            pltpu.VMEM((subjects, 2 * BRICK, LANES), f32),
            pltpu.VMEM((subjects, SLAB_Z, 9, BRICK, LANES), f32),
            pltpu.VMEM((SUB * BRICK, LANES), f32),
            pltpu.VMEM((PARTS, subjects, SUB, BRICK, LANES), bf16),
            pltpu.VMEM((subjects, ROWS, BRICK, LANES), bf16),
            regular((slab_count // CORES,)), regular,
            dma((3,)), dma((BRICK_CHUNKS,)), dma, dma((2 + PARTS,)),
            per_slab, per_slab, per_part, per_part, dma((2,)), dma((2,)),
            dma((subjects,)), dma((subjects,)), dma((PARTS, subjects)), dma((PARTS, subjects)),
        ],
        compiler_params=pltpu.CompilerParams(
            vmem_limit_bytes=32 << 20, collective_id=0, has_side_effects=True
        ),
    )(*arguments)


def solution(mesh):
    in_specs = (
        P("subj", "slab", None),
        P("subj", "slab"),
        P("subj", None, "slab"),
        P("subj", None, "slab", None, None),
    )
    out_specs = P(None, "slab", "subj", None)
    return jax.shard_map(shards, mesh=mesh, in_specs=in_specs, out_specs=out_specs, check_vma=False)
```

```python
import jax
import jax.numpy as jnp
from jax import lax
from jax.experimental import pallas as pl
from jax.experimental.pallas import tpu as pltpu
from jax.sharding import PartitionSpec as P

COMP = 6
BRICK = 16
PAD = 2
EDGE = BRICK + 2 * PAD
ZQ = 4
NEWTON = 2
SLAB_Z = 4
LANES = 128
SUB = 8
ROWS = COMP * SLAB_Z
PARTS = ROWS // SUB
BRICK_ROWS = COMP * EDGE
SPAN = 384
FLAT = BRICK * BRICK
ACROSS = LANES // BRICK
BRICK_CHUNKS = 3
U_ROWS = 3 * (SLAB_Z + 2) * BRICK
U_ALL = U_ROWS + 2 * BRICK
CORES = 2
LEAD = 1


def relayout_groups(x_ref, rows_ref, first_group, groups):
    held = x_ref.shape[0]
    lane = lax.broadcasted_iota(jnp.int32, (held, LANES), 1)
    group_lanes = SUB * EDGE * EDGE

    def step(group, carry):
        for m in range(SUB):
            cz = group * SUB + m
            row = cz % EDGE * COMP + cz // EDGE
            shift = 16 * m
            tiles = []
            for j in range(4):
                first = pl.multiple_of(group * group_lanes + (3 * m + j) * LANES, LANES)
                tile = x_ref[:, pl.ds(first, LANES)].astype(jnp.float32)
                tiles.append(pltpu.roll(tile, LANES - shift, 1) if shift else tile)
            for j in range(4):
                value = tiles[j]
                if shift and j < 3:
                    value = jnp.where(lane < LANES - shift, tiles[j], tiles[j + 1])
                rows_ref[j, pl.ds(row, held, stride=BRICK_ROWS), :] = value
        return carry

    lax.fori_loop(first_group, first_group + groups, step, 0)


def selection():
    source = lax.broadcasted_iota(jnp.int32, (SPAN, FLAT), 0)
    target = lax.broadcasted_iota(jnp.int32, (SPAN, FLAT), 1)
    return (source == target // BRICK * EDGE + target % BRICK).astype(jnp.float32).astype(jnp.bfloat16)


def polar_factor(matrix):
    for newton_step in range(NEWTON):
        cofactor = [
            [
                matrix[(a + 1) % 3][(b + 1) % 3] * matrix[(a + 2) % 3][(b + 2) % 3]
                - matrix[(a + 1) % 3][(b + 2) % 3] * matrix[(a + 2) % 3][(b + 1) % 3]
                for b in range(3)
            ]
            for a in range(3)
        ]
        determinant = (
            matrix[0][0] * cofactor[0][0]
            + matrix[0][1] * cofactor[0][1]
            + matrix[0][2] * cofactor[0][2]
        )
        scaling = 0.5 / determinant
        matrix = [
            [0.5 * matrix[a][b] + cofactor[a][b] * scaling for b in range(3)] for a in range(3)
        ]
    return matrix


def reorient(components, rotation):
    tensor_rows = [
        [components[0], components[3], components[4]],
        [components[3], components[1], components[5]],
        [components[4], components[5], components[2]],
    ]
    left_side = [
        [
            rotation[a][0] * tensor_rows[0][b]
            + rotation[a][1] * tensor_rows[1][b]
            + rotation[a][2] * tensor_rows[2][b]
            for b in range(3)
        ]
        for a in range(3)
    ]
    pair_list = ((0, 0), (1, 1), (2, 2), (0, 1), (0, 2), (1, 2))
    return [
        left_side[a][0] * rotation[b][0]
        + left_side[a][1] * rotation[b][1]
        + left_side[a][2] * rotation[b][2]
        for a, b in pair_list
    ]


def rotation_at(load, halo):
    lane = lax.broadcasted_iota(jnp.int32, (BRICK, LANES), 1)
    sub = lax.broadcasted_iota(jnp.int32, (BRICK, LANES), 0)
    matrix = []
    for a in range(3):
        centre = load(a, 1)
        along_z = (load(a, 2) - load(a, 0)) * 0.5
        below = jnp.where(sub == BRICK - 1, halo(a, 1), pltpu.roll(centre, BRICK - 1, 0))
        above = jnp.where(sub == 0, halo(a, 0), pltpu.roll(centre, 1, 0))
        later = jnp.where(lane == LANES - 1, 0.0, pltpu.roll(centre, LANES - 1, 1))
        earlier = jnp.where(lane == 0, 0.0, pltpu.roll(centre, 1, 1))
        gradients = [along_z, (below - above) * 0.5, (later - earlier) * 0.5]
        gradients[a] = gradients[a] + 1.0
        matrix.append(gradients)
    return polar_factor(matrix)


def slot_tables(ids_ref, offset_ref, held, capacity, me_k):
    pieces = ids_ref.shape[1]
    wanted = ids_ref[...]
    owner, local = wanted // held, wanted % held
    start_z = offset_ref[0] + me_k % ZQ * SLAB_Z
    shift = offset_ref[1] * EDGE + offset_ref[2]
    code = (local * BRICK_ROWS + start_z * COMP) * LANES + shift
    first = lax.broadcasted_iota(jnp.int32, (pieces, pieces), 0)
    second = lax.broadcasted_iota(jnp.int32, (pieces, pieces), 1)

    def upright(row):
        spread = jnp.broadcast_to(row, (pieces, pieces))
        return jnp.sum(jnp.where(first == second, spread, 0), axis=1, keepdims=True)

    owner_up = upright(owner)
    earlier = (owner_up == owner) & (first < second)
    slot = owner * capacity + jnp.sum(earlier.astype(jnp.int32), axis=0, keepdims=True)
    lane = lax.broadcasted_iota(jnp.int32, (pieces, LANES), 1)
    codes = jnp.sum(jnp.where(upright(slot) == lane, upright(code), 0), axis=0, keepdims=True)
    return slot, codes


def warp_kernel(
    ids_hbm, offset_hbm, brick_hbm, u_hbm, out_ref,
    ids_ref, offset_ref, code_ref, slot_row, slot_ref, asked, bricks, rows_ref, stage, crops, arrived_0, arrived_1, arrived_2,
    u_held, edge_out, edge_in, u_out, u_all, halos, rotations, spread, placed, fields,
    seen, opened,
    ids_sem, brick_sem, held_sem, own_sem, ask_send, ask_recv, crop_send, crop_recv, edge_send, edge_recv,
    u_send, u_recv, field_send, field_recv,
):
    count, subjects = asked.shape[0], fields.shape[0]
    chips = count // CORES
    capacity = crops.shape[2]
    height = edge_in.shape[1] // 3
    me_s, me_k = lax.axis_index("subj"), lax.axis_index("slab")
    chip, core = me_k // CORES, me_k % CORES
    sibling = me_k + 1 - 2 * core
    arrived = (arrived_0, arrived_1, arrived_2)
    barrier = pltpu.get_barrier_semaphore()
    has_before, has_after = me_k > 0, me_k < count - 1
    bits = [1 << n for n in range(subjects.bit_length() - 1)]

    def peer_subj(t):
        return (me_s + t) % subjects

    def loop(first, last, step):
        lax.fori_loop(first, last, lambda i, carry: (step(i), carry)[1], 0)

    def each_peer(step):
        loop(1, count, lambda t: step((me_k + t) % count))

    def greet(s, k):
        pl.semaphore_signal(barrier, inc=1, device_id=(s, k), device_id_type=MESH)

    greet(me_s, sibling)
    below = (chip + chips - 1) // chips
    lower = sum((me_s // bit) % 2 for bit in bits)
    pl.semaphore_wait(barrier, 1 + below + lower)

    @pl.when(chip < chips - 1)
    def _():
        greet(me_s, me_k + CORES)

    for bit in bits:
        @pl.when((me_s // bit) % 2 == 0)
        def _():
            greet(me_s + bit, me_k)

    loop(0, chip, lambda c: pl.semaphore_signal(
        seen.at[chip], inc=1, device_id=(me_s, (chip - 1 - c) * CORES + core), device_id_type=MESH
    ))

    @pl.when(me_s == subjects - 1)
    def _():
        for s in range(subjects - 1):
            pl.semaphore_signal(opened, inc=1, device_id=(s, me_k), device_id_type=MESH)

    load_ids = pltpu.make_async_copy(ids_hbm, ids_ref, ids_sem.at[0])
    load_offsets = pltpu.make_async_copy(offset_hbm, offset_ref, ids_sem.at[1])
    load_ids.start()
    load_offsets.start()

    chunk_lanes = brick_hbm.shape[1] // BRICK_CHUNKS

    def load_bricks(c):
        lanes = pl.ds(c * chunk_lanes, chunk_lanes)
        return pltpu.make_async_copy(brick_hbm.at[:, lanes], bricks.at[:, lanes], brick_sem.at[c])

    load_u = pltpu.make_async_copy(u_hbm, u_held, held_sem)
    load_bricks(0).start()
    load_u.start()
    for c in range(1, BRICK_CHUNKS):
        load_bricks(c).start()

    load_ids.wait()
    load_offsets.wait()
    slots, codes = slot_tables(ids_ref, offset_ref, bricks.shape[0], capacity, me_k)
    slot_row[0:1, 0:slots.shape[1]] = slots
    for k in range(count):
        back = (LANES - k * capacity) % LANES
        code_ref[k] = pltpu.roll(codes, back, 1) if back else codes
    load_slots = pltpu.make_async_copy(slot_row, slot_ref, ids_sem.at[2])
    load_slots.start()

    def remote(source, target, send, recv, s, k):
        return pltpu.make_async_remote_copy(
            src_ref=source, dst_ref=target, send_sem=send, recv_sem=recv,
            device_id=(s, k), device_id_type=MESH,
        )

    def ask(k):
        return remote(code_ref.at[k], asked.at[me_k], ask_send, ask_recv.at[me_k], me_s, k)

    def ask_from(k):
        return remote(code_ref.at[k], asked.at[k], ask_send, ask_recv.at[k], me_s, k)

    def ask_chip(c):
        for n in range(CORES):
            ask(c * CORES + n).start()

    loop(0, chip, lambda c: ask_chip(chip - 1 - c))
    ask(sibling).start()
    own_ask = pltpu.make_async_copy(code_ref.at[me_k], asked.at[me_k], own_sem.at[0])
    own_ask.start()

    def ask_above(d):
        @pl.when(chip + d < chips)
        def _():
            pl.semaphore_wait(seen.at[chip + d], 1)
            ask_chip(chip + d)

    load_u.wait()
    for a in range(3):
        for side, z in ((0, SLAB_Z - 1), (1, 0)):
            first = (a * SLAB_Z + z) * height
            edge_out[side, a * height:(a + 1) * height] = u_held[first:first + height].astype(jnp.bfloat16)

    edge_down = remote(edge_out.at[0], edge_in.at[0], edge_send.at[0], edge_recv.at[0], me_s, me_k + 1)
    edge_up = remote(edge_out.at[1], edge_in.at[1], edge_send.at[1], edge_recv.at[1], me_s, me_k - 1)

    @pl.when(has_before)
    def _():
        edge_up.start()

    groups = BRICK_ROWS // SUB // BRICK_CHUNKS
    for c in range(BRICK_CHUNKS):
        load_bricks(c).wait()
        relayout_groups(bricks, rows_ref, c * groups, groups)
        if c < BRICK_CHUNKS - 1:
            ask_above(c + 1)
        if c == 0:
            @pl.when(has_after)
            def _():
                edge_down.start()

    loop(BRICK_CHUNKS, chips, ask_above)
    select = selection()
    lane = lax.broadcasted_iota(jnp.int32, (SUB, LANES), 1)
    own_ask.wait()

    def give(part, k):
        return remote(
            crops.at[part, k], arrived[part].at[pl.ds(me_k * capacity, capacity)],
            crop_send.at[part], crop_recv.at[part], me_s, k,
        )

    def taken(part):
        rows = arrived[part].at[pl.ds(0, (count - 1) * capacity)]
        return remote(rows, rows, crop_send.at[part], crop_recv.at[part], me_s, me_k)

    def given(part):
        rows = crops.at[part, pl.ds(0, count - 1)]
        return remote(rows, rows, crop_send.at[part], crop_recv.at[part], me_s, me_k)

    def cut(code, part):
        start = lax.shift_right_logical(code, 7) + part * SUB
        shift = code & (LANES - 1)
        back = (LANES - shift) & (LANES - 1)
        tiles = [pltpu.roll(rows_ref[j, pl.ds(start, SUB), :], back, 1) for j in range(4)]
        inside = lane < LANES - shift
        return jnp.concatenate([jnp.where(inside, tiles[j], tiles[j + 1]) for j in range(3)], axis=1)

    side = chips // 2
    upper = chip // side
    near_count = side - 1
    outer = 1 - (chip % (chips - 1) + chips - 2) // (chips - 1)

    early = 1 - (1 - outer) * upper

    def far_at(i):
        return i - early * near_count

    def unit_chip(i):
        j = far_at(i)
        far_chip = (1 - upper) * (side + j) + upper * (side - 1 - j)
        step = i - (1 - early) * side
        near_chip = upper * side + (chip - upper * side + 1 + step) % side
        is_far = (j >= 0) & (j < side)
        return jnp.where(i == chips - 1, chip, jnp.where(is_far, far_chip, near_chip))

    def serve(i):
        first_reader = unit_chip(i) * CORES
        j = far_at(i)
        inner_far = (j >= 0) & (j < side)
        leads = inner_far & (j % 2 == 0)
        follows = inner_far & (j % 2 == 1)
        for n in range(CORES):
            k = first_reader + n

            @pl.when(k != me_k)
            def _():
                ask_from(k).wait_recv()

        codes = [
            [asked[first_reader + n, 0, slot] for slot in range(capacity)] for n in range(CORES)
        ]

        def send(part, first):
            for n in range(CORES):
                @pl.when(first + n != me_k)
                def _():
                    give(part, first + n).start()

        for part in range(PARTS):
            for n in range(CORES):
                for pair in range(capacity // 2):
                    both = jnp.concatenate([cut(codes[n][2 * pair + m], part) for m in range(2)], axis=0)
                    row = (n * (capacity // 2) + pair) * 2 * SUB
                    stage[row:row + 2 * SUB, :] = both.astype(jnp.bfloat16)
            found = jnp.dot(stage[...], select, preferred_element_type=jnp.float32)
            for n in range(CORES):
                for slot in range(capacity):
                    first = (n * capacity + slot) * SUB
                    piece = found[first:first + SUB]
                    tile = jnp.concatenate([piece[:, :LANES], piece[:, LANES:]], axis=0)
                    crops[part, first_reader + n, slot] = tile.astype(jnp.bfloat16)
            if part < LEAD:
                send(part, first_reader)
            else:
                @pl.when(jnp.logical_not(leads))
                def _():
                    send(part, first_reader)

        @pl.when(follows)
        def _():
            for part in range(LEAD, PARTS):
                send(part, unit_chip(i - 1) * CORES)

    def u_block(r):
        return remote(u_out.at[r], u_all.at[me_s], u_send, u_recv, r, me_k)

    def u_blocks():
        return remote(
            u_out.at[pl.ds(0, subjects - 1)], u_all.at[pl.ds(0, subjects - 1)], u_send, u_recv, me_s, me_k
        )

    own_u = pltpu.make_async_copy(u_out.at[me_s], u_all.at[me_s], own_sem.at[1 + PARTS])

    def hand_u():
        @pl.when(has_before)
        def _():
            edge_down_in = remote(edge_out.at[0], edge_in.at[0], edge_send.at[0], edge_recv.at[0], me_s, me_k - 1)
            edge_down_in.wait_recv()

        @pl.when(me_k == 0)
        def _():
            edge_in[0] = jnp.zeros(edge_in.shape[1:], jnp.bfloat16)

        @pl.when(has_after)
        def _():
            edge_up_in = remote(edge_out.at[1], edge_in.at[1], edge_send.at[1], edge_recv.at[1], me_s, me_k + 1)
            edge_up_in.wait_recv()

        @pl.when(me_k == count - 1)
        def _():
            edge_in[1] = jnp.zeros(edge_in.shape[1:], jnp.bfloat16)

        blank = jnp.zeros((BRICK - 3 * SLAB_Z, LANES), jnp.float32)
        none = jnp.zeros((3 * SLAB_Z, LANES), jnp.float32)
        for r in range(subjects):
            for a in range(3):
                for z in range(SLAB_Z + 2):
                    to = (a * (SLAB_Z + 2) + z) * BRICK
                    if z == 0 or z == SLAB_Z + 1:
                        first = a * height + r * BRICK
                        block = edge_in[min(z, 1), first:first + BRICK]
                    else:
                        first = (a * SLAB_Z + z - 1) * height + r * BRICK
                        block = u_held[first:first + BRICK].astype(jnp.bfloat16)
                    u_out[r, to:to + BRICK] = block
            top, bottom = none, none
            if r > 0:
                top = u_held[pl.ds(r * BRICK - 1, 3 * SLAB_Z, stride=height), :]
            if r < subjects - 1:
                bottom = u_held[pl.ds((r + 1) * BRICK, 3 * SLAB_Z, stride=height), :]
            u_out[r, U_ROWS:U_ALL] = jnp.concatenate([top, blank, bottom, blank], axis=0).astype(jnp.bfloat16)

        @pl.when(me_s < subjects - 1)
        def _():
            pl.semaphore_wait(opened, 1)

        for t in range(1, subjects):
            u_block(peer_subj(t)).start()
        own_u.start()

    def serve_and_hand(i):
        serve(i)

        @pl.when(i == (1 - outer) * (1 + early))
        def _():
            hand_u()

    loop(0, chips, serve_and_hand)

    def keep(part):
        return pltpu.make_async_copy(
            crops.at[part, me_k], arrived[part].at[pl.ds(me_k * capacity, capacity)], own_sem.at[1 + part]
        )

    for part in range(PARTS):
        keep(part).start()

    own_u.wait()
    u_blocks().wait_recv()
    for s in range(subjects):
        halos[s] = u_all[s, U_ROWS:U_ALL].astype(jnp.float32)

    def rotate(at, carry):
        s, z = at // SLAB_Z, at % SLAB_Z

        def load(a, dz):
            first = pl.multiple_of((a * (SLAB_Z + 2) + z + dz) * BRICK, BRICK)
            return u_all[s, pl.ds(first, BRICK), :].astype(jnp.float32)

        def halo(a, side):
            return halos[s, pl.ds(side * BRICK + a * SLAB_Z + z, 1), :]

        rotation = rotation_at(load, halo)
        for a in range(3):
            for b in range(3):
                rotations[s, z, a * 3 + b] = rotation[a][b]
        return carry

    lax.fori_loop(0, subjects * SLAB_Z, rotate, 0)

    group = lax.broadcasted_iota(jnp.int32, (SUB, LANES), 1) // BRICK

    def place(part, r):
        halves = [[], []]
        for j in range(ACROSS):
            tile = arrived[part][slot_ref[0, r * ACROSS + j]].astype(jnp.float32)
            halves[0].append(tile[:SUB])
            halves[1].append(tile[SUB:])
        for h in range(2):
            pieces = halves[h]
            for bit in (1, 2, 4):
                upper = (group & bit) != 0
                moved = list(pieces)
                for j in range(ACROSS):
                    if j & bit:
                        continue
                    first, second = pieces[j], pieces[j | bit]
                    moved[j] = jnp.where(upper, pltpu.roll(second, BRICK * bit, 1), first)
                    moved[j | bit] = jnp.where(upper, second, pltpu.roll(first, LANES - BRICK * bit, 1))
                pieces = moved
            for y in range(SUB):
                spread[pl.ds(h * SUB + y, SUB, stride=BRICK), :] = pieces[y]
        return spread[...].astype(jnp.bfloat16).reshape(SUB, BRICK, LANES)

    def share(part, r):
        return remote(
            placed.at[part, r], fields.at[me_s, pl.ds(part * SUB, SUB)],
            field_send.at[part], field_recv.at[part, me_s], r, me_k,
        )

    def shared_from(part, s):
        return remote(
            placed.at[part, s], fields.at[s, pl.ds(part * SUB, SUB)],
            field_send.at[part], field_recv.at[part, s], s, me_k,
        )

    def other(t):
        return t - 1 + (t - 1 + subjects - me_s) // subjects

    def combine(z, s, starts):
        rotation = [[rotations[s, z, a * 3 + b] for b in range(3)] for a in range(3)]
        tensor = [
            fields[s, z * COMP + c].astype(jnp.float32) * (1.0 / subjects) for c in range(COMP)
        ]
        rotated = reorient(tensor, rotation)
        for c in range(COMP):
            out_ref[c, z] = rotated[c] if starts else out_ref[c, z] + rotated[c]

    def combine_part(part, s, starts):
        for z in range(SLAB_Z):
            if part * SUB < (z + 1) * COMP <= (part + 1) * SUB:
                combine(z, s, starts)

    def finish_part(part):
        combine_part(part, me_s, True)
        for t in range(1, subjects):
            shared_from(part, other(t)).wait_recv()
            combine_part(part, other(t), False)

    load_slots.wait()
    for part in range(PARTS):
        keep(part).wait()
        taken(part).wait_recv()

        def place_and_share(t, carry):
            r = other(t)
            placed[part, r] = place(part, r)
            share(part, r).start()
            return carry

        lax.fori_loop(1, subjects, place_and_share, 0)
        fields[me_s, part * SUB:(part + 1) * SUB] = place(part, me_s)
        if part > 0:
            finish_part(part - 1)

    told = code_ref.at[pl.ds(0, count - 1)]
    remote(told, told, ask_send, ask_recv.at[me_k], me_s, me_k).wait_send()
    for part in range(PARTS):
        given(part).wait_send()
    u_blocks().wait_send()

    @pl.when(has_after)
    def _():
        edge_down.wait_send()

    @pl.when(has_before)
    def _():
        edge_up.wait_send()

    for part in range(PARTS):
        rows = placed.at[part, pl.ds(0, subjects - 1)]
        remote(rows, rows, field_send.at[part], field_recv.at[part, me_s], me_s, me_k).wait_send()
    finish_part(PARTS - 1)


MESH = pl.DeviceIdType.MESH
VMEM_SPEC = pl.BlockSpec(memory_space=pltpu.VMEM)
HBM_SPEC = pl.BlockSpec(memory_space=pl.ANY)


def shards(source_bricks, brick_ids, brick_offsets, deformation):
    slab_count, subjects = lax.axis_size("slab"), lax.axis_size("subj")
    pieces = brick_ids.shape[1]
    held = source_bricks.shape[1]
    height = deformation.shape[3]
    capacity = max(2, 3 * pieces // (2 * slab_count))
    arguments = [
        brick_ids, brick_offsets.reshape(3, 1, pieces), source_bricks[0],
        deformation[0].reshape(-1, LANES),
    ]
    arguments = [pltpu.with_memory_space_constraint(x, pltpu.HBM) for x in arguments]
    bf16, f32, dma = jnp.bfloat16, jnp.float32, pltpu.SemaphoreType.DMA
    regular = pltpu.SemaphoreType.REGULAR
    per_slab, per_part = dma((slab_count,)), dma((PARTS,))
    return pl.pallas_call(
        warp_kernel,
        out_shape=jax.ShapeDtypeStruct((COMP, SLAB_Z, BRICK, LANES), f32),
        in_specs=[HBM_SPEC] * 4,
        out_specs=VMEM_SPEC,
        scratch_shapes=[
            pltpu.VMEM((1, pieces), jnp.int32),
            pltpu.VMEM((3, 1, pieces), jnp.int32),
            pltpu.VMEM((slab_count, 1, LANES), jnp.int32),
            pltpu.VMEM((1, LANES), jnp.int32),
            pltpu.SMEM((1, LANES), jnp.int32),
            pltpu.VMEM((slab_count, 1, LANES), jnp.int32),
            pltpu.VMEM((held, source_bricks.shape[2]), bf16),
            pltpu.VMEM((4, held * BRICK_ROWS, LANES), f32),
            pltpu.VMEM((CORES * capacity * SUB, SPAN), bf16),
            pltpu.VMEM((PARTS, slab_count, capacity, BRICK, LANES), bf16),
            *[pltpu.VMEM((slab_count * capacity, BRICK, LANES), bf16)] * PARTS,
            pltpu.VMEM((3 * SLAB_Z * height, LANES), f32),
            pltpu.VMEM((2, 3 * height, LANES), bf16),
            pltpu.VMEM((2, 3 * height, LANES), bf16),
            pltpu.VMEM((subjects, U_ALL, LANES), bf16),
            pltpu.VMEM((subjects, U_ALL, LANES), bf16),
            pltpu.VMEM((subjects, 2 * BRICK, LANES), f32),
            pltpu.VMEM((subjects, SLAB_Z, 9, BRICK, LANES), f32),
            pltpu.VMEM((SUB * BRICK, LANES), f32),
            pltpu.VMEM((PARTS, subjects, SUB, BRICK, LANES), bf16),
            pltpu.VMEM((subjects, ROWS, BRICK, LANES), bf16),
            regular((slab_count // CORES,)), regular,
            dma((3,)), dma((BRICK_CHUNKS,)), dma, dma((2 + PARTS,)),
            dma, per_slab, per_part, per_part, dma((2,)), dma((2,)),
            dma, dma, per_part, dma((PARTS, subjects)),
        ],
        compiler_params=pltpu.CompilerParams(
            vmem_limit_bytes=32 << 20, collective_id=0, has_side_effects=True
        ),
    )(*arguments)


def solution(mesh):
    in_specs = (
        P("subj", "slab", None),
        P("subj", "slab"),
        P("subj", None, "slab"),
        P("subj", None, "slab", None, None),
    )
    out_specs = P(None, "slab", "subj", None)
    return jax.shard_map(shards, mesh=mesh, in_specs=in_specs, out_specs=out_specs, check_vma=False)
```

```python
import jax
import jax.numpy as jnp
from jax import lax
from jax.experimental import pallas as pl
from jax.experimental.pallas import tpu as pltpu
from jax.sharding import PartitionSpec as P

COMP = 6
BRICK = 16
PAD = 2
EDGE = BRICK + 2 * PAD
ZQ = 4
NEWTON = 2
SLAB_Z = 4
LANES = 128
SUB = 8
ROWS = COMP * SLAB_Z
PARTS = ROWS // SUB
BRICK_ROWS = COMP * EDGE
SPAN = 384
FLAT = BRICK * BRICK
ACROSS = LANES // BRICK
BRICK_CHUNKS = 3
U_ROWS = 3 * (SLAB_Z + 2) * BRICK
U_ALL = U_ROWS + 2 * BRICK
CORES = 2
LEAD = 1


def relayout_groups(x_ref, rows_ref, first_group, groups):
    held = x_ref.shape[0]
    lane = lax.broadcasted_iota(jnp.int32, (held, LANES), 1)
    group_lanes = SUB * EDGE * EDGE

    def step(group, carry):
        for m in range(SUB):
            cz = group * SUB + m
            row = cz % EDGE * COMP + cz // EDGE
            shift = 16 * m
            tiles = []
            for j in range(4):
                first = pl.multiple_of(group * group_lanes + (3 * m + j) * LANES, LANES)
                tile = x_ref[:, pl.ds(first, LANES)].astype(jnp.float32)
                tiles.append(pltpu.roll(tile, LANES - shift, 1) if shift else tile)
            for j in range(4):
                value = tiles[j]
                if shift and j < 3:
                    value = jnp.where(lane < LANES - shift, tiles[j], tiles[j + 1])
                rows_ref[j, pl.ds(row, held, stride=BRICK_ROWS), :] = value
        return carry

    lax.fori_loop(first_group, first_group + groups, step, 0)


def selection():
    source = lax.broadcasted_iota(jnp.int32, (SPAN, FLAT), 0)
    target = lax.broadcasted_iota(jnp.int32, (SPAN, FLAT), 1)
    return (source == target // BRICK * EDGE + target % BRICK).astype(jnp.float32).astype(jnp.bfloat16)


def polar_factor(matrix):
    for newton_step in range(NEWTON):
        cofactor = [
            [
                matrix[(a + 1) % 3][(b + 1) % 3] * matrix[(a + 2) % 3][(b + 2) % 3]
                - matrix[(a + 1) % 3][(b + 2) % 3] * matrix[(a + 2) % 3][(b + 1) % 3]
                for b in range(3)
            ]
            for a in range(3)
        ]
        determinant = (
            matrix[0][0] * cofactor[0][0]
            + matrix[0][1] * cofactor[0][1]
            + matrix[0][2] * cofactor[0][2]
        )
        scaling = 0.5 / determinant
        matrix = [
            [0.5 * matrix[a][b] + cofactor[a][b] * scaling for b in range(3)] for a in range(3)
        ]
    return matrix


def reorient(components, rotation):
    tensor_rows = [
        [components[0], components[3], components[4]],
        [components[3], components[1], components[5]],
        [components[4], components[5], components[2]],
    ]
    left_side = [
        [
            rotation[a][0] * tensor_rows[0][b]
            + rotation[a][1] * tensor_rows[1][b]
            + rotation[a][2] * tensor_rows[2][b]
            for b in range(3)
        ]
        for a in range(3)
    ]
    pair_list = ((0, 0), (1, 1), (2, 2), (0, 1), (0, 2), (1, 2))
    return [
        left_side[a][0] * rotation[b][0]
        + left_side[a][1] * rotation[b][1]
        + left_side[a][2] * rotation[b][2]
        for a, b in pair_list
    ]


def rotation_at(load, halo):
    lane = lax.broadcasted_iota(jnp.int32, (BRICK, LANES), 1)
    sub = lax.broadcasted_iota(jnp.int32, (BRICK, LANES), 0)
    matrix = []
    for a in range(3):
        centre = load(a, 1)
        along_z = (load(a, 2) - load(a, 0)) * 0.5
        below = jnp.where(sub == BRICK - 1, halo(a, 1), pltpu.roll(centre, BRICK - 1, 0))
        above = jnp.where(sub == 0, halo(a, 0), pltpu.roll(centre, 1, 0))
        later = jnp.where(lane == LANES - 1, 0.0, pltpu.roll(centre, LANES - 1, 1))
        earlier = jnp.where(lane == 0, 0.0, pltpu.roll(centre, 1, 1))
        gradients = [along_z, (below - above) * 0.5, (later - earlier) * 0.5]
        gradients[a] = gradients[a] + 1.0
        matrix.append(gradients)
    return polar_factor(matrix)


def slot_tables(ids_ref, offset_ref, held, capacity, me_k):
    pieces = ids_ref.shape[1]
    wanted = ids_ref[...]
    owner, local = wanted // held, wanted % held
    start_z = offset_ref[0] + me_k % ZQ * SLAB_Z
    shift = offset_ref[1] * EDGE + offset_ref[2]
    code = (local * BRICK_ROWS + start_z * COMP) * LANES + shift
    first = lax.broadcasted_iota(jnp.int32, (pieces, pieces), 0)
    second = lax.broadcasted_iota(jnp.int32, (pieces, pieces), 1)

    def upright(row):
        spread = jnp.broadcast_to(row, (pieces, pieces))
        return jnp.sum(jnp.where(first == second, spread, 0), axis=1, keepdims=True)

    owner_up = upright(owner)
    earlier = (owner_up == owner) & (first < second)
    slot = owner * capacity + jnp.sum(earlier.astype(jnp.int32), axis=0, keepdims=True)
    lane = lax.broadcasted_iota(jnp.int32, (pieces, LANES), 1)
    codes = jnp.sum(jnp.where(upright(slot) == lane, upright(code), 0), axis=0, keepdims=True)
    return slot, codes


def warp_kernel(
    ids_hbm, offset_hbm, brick_hbm, u_hbm, out_ref,
    ids_ref, offset_ref, code_ref, slot_row, slot_ref, asked, bricks, rows_ref, stage, crops, arrived_0, arrived_1, arrived_2,
    u_held, edge_out, edge_in, u_out, u_all, halos, rotations, spread, placed, fields,
    seen, opened,
    ids_sem, brick_sem, held_sem, own_sem, ask_send, ask_recv, crop_send, crop_recv, edge_send, edge_recv,
    u_send, u_recv, field_send, field_recv,
):
    count, subjects = asked.shape[0], fields.shape[0]
    chips = count // CORES
    capacity = crops.shape[2]
    height = edge_in.shape[1] // 3
    me_s, me_k = lax.axis_index("subj"), lax.axis_index("slab")
    chip, core = me_k // CORES, me_k % CORES
    sibling = me_k + 1 - 2 * core
    side_low = chips // 2
    arrived = (arrived_0, arrived_1, arrived_2)
    barrier = pltpu.get_barrier_semaphore()
    has_before, has_after = me_k > 0, me_k < count - 1
    bits = [1 << n for n in range(subjects.bit_length() - 1)]

    def peer_subj(t):
        return (me_s + t) % subjects

    def loop(first, last, step):
        lax.fori_loop(first, last, lambda i, carry: (step(i), carry)[1], 0)

    def each_peer(step):
        loop(1, count, lambda t: step((me_k + t) % count))

    def greet(s, k):
        pl.semaphore_signal(barrier, inc=1, device_id=(s, k), device_id_type=MESH)

    greet(me_s, sibling)
    below = (chip + chips - 1) // chips
    lower = sum((me_s // bit) % 2 for bit in bits)
    pl.semaphore_wait(barrier, 1 + below + lower)

    @pl.when(chip < chips - 1)
    def _():
        greet(me_s, me_k + CORES)

    for bit in bits:
        @pl.when((me_s // bit) % 2 == 0)
        def _():
            greet(me_s + bit, me_k)

    loop(0, chip, lambda c: pl.semaphore_signal(
        seen.at[chip], inc=1, device_id=(me_s, (chip - 1 - c) * CORES + core), device_id_type=MESH
    ))

    @pl.when(me_s == subjects - 1)
    def _():
        for s in range(subjects - 1):
            pl.semaphore_signal(opened, inc=1, device_id=(s, me_k), device_id_type=MESH)

    load_ids = pltpu.make_async_copy(ids_hbm, ids_ref, ids_sem.at[0])
    load_offsets = pltpu.make_async_copy(offset_hbm, offset_ref, ids_sem.at[1])
    load_ids.start()
    load_offsets.start()

    chunk_lanes = brick_hbm.shape[1] // BRICK_CHUNKS

    def load_bricks(c):
        lanes = pl.ds(c * chunk_lanes, chunk_lanes)
        return pltpu.make_async_copy(brick_hbm.at[:, lanes], bricks.at[:, lanes], brick_sem.at[c])

    load_u = pltpu.make_async_copy(u_hbm, u_held, held_sem)
    load_bricks(0).start()
    load_u.start()
    for c in range(1, BRICK_CHUNKS):
        load_bricks(c).start()

    load_ids.wait()
    load_offsets.wait()
    slots, codes = slot_tables(ids_ref, offset_ref, bricks.shape[0], capacity, me_k)
    slot_row[0:1, 0:slots.shape[1]] = slots
    for k in range(count):
        back = (LANES - k * capacity) % LANES
        code_ref[k] = pltpu.roll(codes, back, 1) if back else codes
    load_slots = pltpu.make_async_copy(slot_row, slot_ref, ids_sem.at[2])
    load_slots.start()

    def remote(source, target, send, recv, s, k):
        return pltpu.make_async_remote_copy(
            src_ref=source, dst_ref=target, send_sem=send, recv_sem=recv,
            device_id=(s, k), device_id_type=MESH,
        )

    def ask(k):
        return remote(code_ref.at[k], asked.at[me_k], ask_send, ask_recv.at[me_k], me_s, k)

    def ask_from(k):
        return remote(code_ref.at[k], asked.at[k], ask_send, ask_recv.at[k], me_s, k)

    def ask_chip(c):
        for n in range(CORES):
            ask(c * CORES + n).start()

    loop(0, chip, lambda c: ask_chip(chip - 1 - c))
    ask(sibling).start()
    own_ask = pltpu.make_async_copy(code_ref.at[me_k], asked.at[me_k], own_sem.at[0])
    own_ask.start()

    def ask_above(d):
        @pl.when(chip + d < chips)
        def _():
            pl.semaphore_wait(seen.at[chip + d], 1)
            ask_chip(chip + d)

    load_u.wait()
    for a in range(3):
        for side, z in ((0, SLAB_Z - 1), (1, 0)):
            first = (a * SLAB_Z + z) * height
            edge_out[side, a * height:(a + 1) * height] = u_held[first:first + height].astype(jnp.bfloat16)

    edge_down = remote(edge_out.at[0], edge_in.at[0], edge_send.at[0], edge_recv.at[0], me_s, me_k + 1)
    edge_up = remote(edge_out.at[1], edge_in.at[1], edge_send.at[1], edge_recv.at[1], me_s, me_k - 1)

    @pl.when(has_before)
    def _():
        edge_up.start()

    @pl.when(chip < side_low)
    def _():
        ask_above(1)

    groups = BRICK_ROWS // SUB // BRICK_CHUNKS
    for c in range(BRICK_CHUNKS):
        load_bricks(c).wait()
        relayout_groups(bricks, rows_ref, c * groups, groups)
        if c == 0:
            @pl.when(chip >= side_low)
            def _():
                ask_above(1)
        elif c < BRICK_CHUNKS - 1:
            ask_above(c + 1)
        if c == 0:
            @pl.when(has_after)
            def _():
                edge_down.start()

    loop(BRICK_CHUNKS, chips, ask_above)
    select = selection()
    lane = lax.broadcasted_iota(jnp.int32, (SUB, LANES), 1)
    own_ask.wait()

    def give(part, k):
        return remote(
            crops.at[part, k], arrived[part].at[pl.ds(me_k * capacity, capacity)],
            crop_send.at[part], crop_recv.at[part], me_s, k,
        )

    def taken(part):
        rows = arrived[part].at[pl.ds(0, (count - 1) * capacity)]
        return remote(rows, rows, crop_send.at[part], crop_recv.at[part], me_s, me_k)

    def given(part):
        rows = crops.at[part, pl.ds(0, count - 1)]
        return remote(rows, rows, crop_send.at[part], crop_recv.at[part], me_s, me_k)

    def cut(code, part):
        start = lax.shift_right_logical(code, 7) + part * SUB
        shift = code & (LANES - 1)
        back = (LANES - shift) & (LANES - 1)
        tiles = [pltpu.roll(rows_ref[j, pl.ds(start, SUB), :], back, 1) for j in range(4)]
        inside = lane < LANES - shift
        return jnp.concatenate([jnp.where(inside, tiles[j], tiles[j + 1]) for j in range(3)], axis=1)

    side = chips // 2
    upper = chip // side
    near_count = side - 1
    outer = 1 - (chip % (chips - 1) + chips - 2) // (chips - 1)

    early = 1 - (1 - outer) * upper

    def far_at(i):
        return i - early * near_count

    def unit_chip(i):
        j = far_at(i)
        far_chip = (1 - upper) * (side + j) + upper * (side - 1 - j)
        step = i - (1 - early) * side
        near_chip = upper * side + (chip - upper * side + 1 + step) % side
        is_far = (j >= 0) & (j < side)
        return jnp.where(i == chips - 1, chip, jnp.where(is_far, far_chip, near_chip))

    def serve(i):
        first_reader = unit_chip(i) * CORES
        j = far_at(i)
        inner_far = (j >= 0) & (j < side)
        leads = inner_far & (j % 2 == 0)
        follows = inner_far & (j % 2 == 1)
        for n in range(CORES):
            k = first_reader + n

            @pl.when(k != me_k)
            def _():
                ask_from(k).wait_recv()

        codes = [
            [asked[first_reader + n, 0, slot] for slot in range(capacity)] for n in range(CORES)
        ]

        def send(part, first):
            for n in range(CORES):
                @pl.when(first + n != me_k)
                def _():
                    give(part, first + n).start()

        for part in range(PARTS):
            for n in range(CORES):
                for pair in range(capacity // 2):
                    both = jnp.concatenate([cut(codes[n][2 * pair + m], part) for m in range(2)], axis=0)
                    row = (n * (capacity // 2) + pair) * 2 * SUB
                    stage[row:row + 2 * SUB, :] = both.astype(jnp.bfloat16)
            found = jnp.dot(stage[...], select, preferred_element_type=jnp.float32)
            for n in range(CORES):
                for slot in range(capacity):
                    first = (n * capacity + slot) * SUB
                    piece = found[first:first + SUB]
                    tile = jnp.concatenate([piece[:, :LANES], piece[:, LANES:]], axis=0)
                    crops[part, first_reader + n, slot] = tile.astype(jnp.bfloat16)
            if part < LEAD:
                send(part, first_reader)
            else:
                @pl.when(jnp.logical_not(leads))
                def _():
                    send(part, first_reader)

        @pl.when(follows)
        def _():
            for part in range(LEAD, PARTS):
                send(part, unit_chip(i - 1) * CORES)

    def u_block(r):
        return remote(u_out.at[r], u_all.at[me_s], u_send, u_recv, r, me_k)

    def u_blocks():
        return remote(
            u_out.at[pl.ds(0, subjects - 1)], u_all.at[pl.ds(0, subjects - 1)], u_send, u_recv, me_s, me_k
        )

    own_u = pltpu.make_async_copy(u_out.at[me_s], u_all.at[me_s], own_sem.at[1 + PARTS])

    def hand_u():
        @pl.when(has_before)
        def _():
            edge_down_in = remote(edge_out.at[0], edge_in.at[0], edge_send.at[0], edge_recv.at[0], me_s, me_k - 1)
            edge_down_in.wait_recv()

        @pl.when(me_k == 0)
        def _():
            edge_in[0] = jnp.zeros(edge_in.shape[1:], jnp.bfloat16)

        @pl.when(has_after)
        def _():
            edge_up_in = remote(edge_out.at[1], edge_in.at[1], edge_send.at[1], edge_recv.at[1], me_s, me_k + 1)
            edge_up_in.wait_recv()

        @pl.when(me_k == count - 1)
        def _():
            edge_in[1] = jnp.zeros(edge_in.shape[1:], jnp.bfloat16)

        blank = jnp.zeros((BRICK - 3 * SLAB_Z, LANES), jnp.float32)
        none = jnp.zeros((3 * SLAB_Z, LANES), jnp.float32)
        for r in range(subjects):
            for a in range(3):
                for z in range(SLAB_Z + 2):
                    to = (a * (SLAB_Z + 2) + z) * BRICK
                    if z == 0 or z == SLAB_Z + 1:
                        first = a * height + r * BRICK
                        block = edge_in[min(z, 1), first:first + BRICK]
                    else:
                        first = (a * SLAB_Z + z - 1) * height + r * BRICK
                        block = u_held[first:first + BRICK].astype(jnp.bfloat16)
                    u_out[r, to:to + BRICK] = block
            top, bottom = none, none
            if r > 0:
                top = u_held[pl.ds(r * BRICK - 1, 3 * SLAB_Z, stride=height), :]
            if r < subjects - 1:
                bottom = u_held[pl.ds((r + 1) * BRICK, 3 * SLAB_Z, stride=height), :]
            u_out[r, U_ROWS:U_ALL] = jnp.concatenate([top, blank, bottom, blank], axis=0).astype(jnp.bfloat16)

        @pl.when(me_s < subjects - 1)
        def _():
            pl.semaphore_wait(opened, 1)

        for t in range(1, subjects):
            u_block(peer_subj(t)).start()
        own_u.start()

    def serve_and_hand(i):
        serve(i)

        @pl.when(i == (1 - outer) * (1 + early))
        def _():
            hand_u()

    loop(0, chips, serve_and_hand)

    def keep(part):
        return pltpu.make_async_copy(
            crops.at[part, me_k], arrived[part].at[pl.ds(me_k * capacity, capacity)], own_sem.at[1 + part]
        )

    for part in range(PARTS):
        keep(part).start()

    own_u.wait()
    u_blocks().wait_recv()
    for s in range(subjects):
        halos[s] = u_all[s, U_ROWS:U_ALL].astype(jnp.float32)

    def rotate(at, carry):
        s, z = at // SLAB_Z, at % SLAB_Z

        def load(a, dz):
            first = pl.multiple_of((a * (SLAB_Z + 2) + z + dz) * BRICK, BRICK)
            return u_all[s, pl.ds(first, BRICK), :].astype(jnp.float32)

        def halo(a, side):
            return halos[s, pl.ds(side * BRICK + a * SLAB_Z + z, 1), :]

        rotation = rotation_at(load, halo)
        for a in range(3):
            for b in range(3):
                rotations[s, z, a * 3 + b] = rotation[a][b]
        return carry

    lax.fori_loop(0, subjects * SLAB_Z, rotate, 0)

    group = lax.broadcasted_iota(jnp.int32, (SUB, LANES), 1) // BRICK

    def place(part, r):
        halves = [[], []]
        for j in range(ACROSS):
            tile = arrived[part][slot_ref[0, r * ACROSS + j]].astype(jnp.float32)
            halves[0].append(tile[:SUB])
            halves[1].append(tile[SUB:])
        for h in range(2):
            pieces = halves[h]
            for bit in (1, 2, 4):
                upper = (group & bit) != 0
                moved = list(pieces)
                for j in range(ACROSS):
                    if j & bit:
                        continue
                    first, second = pieces[j], pieces[j | bit]
                    moved[j] = jnp.where(upper, pltpu.roll(second, BRICK * bit, 1), first)
                    moved[j | bit] = jnp.where(upper, second, pltpu.roll(first, LANES - BRICK * bit, 1))
                pieces = moved
            for y in range(SUB):
                spread[pl.ds(h * SUB + y, SUB, stride=BRICK), :] = pieces[y]
        return spread[...].astype(jnp.bfloat16).reshape(SUB, BRICK, LANES)

    def share(part, r):
        return remote(
            placed.at[part, r], fields.at[me_s, pl.ds(part * SUB, SUB)],
            field_send.at[part], field_recv.at[part, me_s], r, me_k,
        )

    def shared_from(part, s):
        return remote(
            placed.at[part, s], fields.at[s, pl.ds(part * SUB, SUB)],
            field_send.at[part], field_recv.at[part, s], s, me_k,
        )

    def other(t):
        return t - 1 + (t - 1 + subjects - me_s) // subjects

    def combine(z, s, starts):
        rotation = [[rotations[s, z, a * 3 + b] for b in range(3)] for a in range(3)]
        tensor = [
            fields[s, z * COMP + c].astype(jnp.float32) for c in range(COMP)
        ]
        rotated = reorient(tensor, rotation)
        for c in range(COMP):
            out_ref[c, z] = rotated[c] if starts else out_ref[c, z] + rotated[c]

    def combine_part(part, s, starts):
        for z in range(SLAB_Z):
            if part * SUB < (z + 1) * COMP <= (part + 1) * SUB:
                combine(z, s, starts)

    def finish_part(part):
        combine_part(part, me_s, True)
        for t in range(1, subjects):
            shared_from(part, other(t)).wait_recv()
            combine_part(part, other(t), False)

    load_slots.wait()
    for part in range(PARTS):
        keep(part).wait()
        taken(part).wait_recv()

        def place_and_share(t, carry):
            r = other(t)
            placed[part, r] = place(part, r)
            share(part, r).start()
            return carry

        lax.fori_loop(1, subjects, place_and_share, 0)
        fields[me_s, part * SUB:(part + 1) * SUB] = place(part, me_s)
        if part > 0:
            finish_part(part - 1)

    told = code_ref.at[pl.ds(0, count - 1)]
    remote(told, told, ask_send, ask_recv.at[me_k], me_s, me_k).wait_send()
    for part in range(PARTS):
        given(part).wait_send()
    u_blocks().wait_send()

    @pl.when(has_after)
    def _():
        edge_down.wait_send()

    @pl.when(has_before)
    def _():
        edge_up.wait_send()

    for part in range(PARTS):
        rows = placed.at[part, pl.ds(0, subjects - 1)]
        remote(rows, rows, field_send.at[part], field_recv.at[part, me_s], me_s, me_k).wait_send()
    finish_part(PARTS - 1)


MESH = pl.DeviceIdType.MESH
VMEM_SPEC = pl.BlockSpec(memory_space=pltpu.VMEM)
HBM_SPEC = pl.BlockSpec(memory_space=pl.ANY)


def shards(source_bricks, brick_ids, brick_offsets, deformation):
    slab_count, subjects = lax.axis_size("slab"), lax.axis_size("subj")
    pieces = brick_ids.shape[1]
    held = source_bricks.shape[1]
    height = deformation.shape[3]
    capacity = max(2, 3 * pieces // (2 * slab_count))
    arguments = [
        brick_ids, brick_offsets.reshape(3, 1, pieces), source_bricks[0],
        deformation[0].reshape(-1, LANES),
    ]
    arguments = [pltpu.with_memory_space_constraint(x, pltpu.HBM) for x in arguments]
    bf16, f32, dma = jnp.bfloat16, jnp.float32, pltpu.SemaphoreType.DMA
    regular = pltpu.SemaphoreType.REGULAR
    per_slab, per_part = dma((slab_count,)), dma((PARTS,))
    total = pl.pallas_call(
        warp_kernel,
        out_shape=jax.ShapeDtypeStruct((COMP, SLAB_Z, BRICK, LANES), f32),
        in_specs=[HBM_SPEC] * 4,
        out_specs=VMEM_SPEC,
        scratch_shapes=[
            pltpu.VMEM((1, pieces), jnp.int32),
            pltpu.VMEM((3, 1, pieces), jnp.int32),
            pltpu.VMEM((slab_count, 1, LANES), jnp.int32),
            pltpu.VMEM((1, LANES), jnp.int32),
            pltpu.SMEM((1, LANES), jnp.int32),
            pltpu.VMEM((slab_count, 1, LANES), jnp.int32),
            pltpu.VMEM((held, source_bricks.shape[2]), bf16),
            pltpu.VMEM((4, held * BRICK_ROWS, LANES), f32),
            pltpu.VMEM((CORES * capacity * SUB, SPAN), bf16),
            pltpu.VMEM((PARTS, slab_count, capacity, BRICK, LANES), bf16),
            *[pltpu.VMEM((slab_count * capacity, BRICK, LANES), bf16)] * PARTS,
            pltpu.VMEM((3 * SLAB_Z * height, LANES), f32),
            pltpu.VMEM((2, 3 * height, LANES), bf16),
            pltpu.VMEM((2, 3 * height, LANES), bf16),
            pltpu.VMEM((subjects, U_ALL, LANES), bf16),
            pltpu.VMEM((subjects, U_ALL, LANES), bf16),
            pltpu.VMEM((subjects, 2 * BRICK, LANES), f32),
            pltpu.VMEM((subjects, SLAB_Z, 9, BRICK, LANES), f32),
            pltpu.VMEM((SUB * BRICK, LANES), f32),
            pltpu.VMEM((PARTS, subjects, SUB, BRICK, LANES), bf16),
            pltpu.VMEM((subjects, ROWS, BRICK, LANES), bf16),
            regular((slab_count // CORES,)), regular,
            dma((3,)), dma((BRICK_CHUNKS,)), dma, dma((2 + PARTS,)),
            dma, per_slab, per_part, per_part, dma((2,)), dma((2,)),
            dma, dma, per_part, dma((PARTS, subjects)),
        ],
        compiler_params=pltpu.CompilerParams(
            vmem_limit_bytes=32 << 20, collective_id=0, has_side_effects=True
        ),
    )(*arguments)
    return total * (1.0 / subjects)


def solution(mesh):
    in_specs = (
        P("subj", "slab", None),
        P("subj", "slab"),
        P("subj", None, "slab"),
        P("subj", None, "slab", None, None),
    )
    out_specs = P(None, "slab", "subj", None)
    return jax.shard_map(shards, mesh=mesh, in_specs=in_specs, out_specs=out_specs, check_vma=False)
```
